128 devices in a mesh: feat: 64 (over z, x, y), frame: 2 (over core).
Axes of the slice: x: 4, y: 4, z: 4, core: 2. Of those that a mesh axis runs over, the one named last changes fastest.
Arguments:
- frames: float32 [6144, 440], P(('frame', 'feat')), may hold values from -6 to 6
- labels: int32 [6144], P('frame'), may hold values from 0 to 146, as said below
- proj: float32 [440, 131072], P(None, 'feat'), may hold values from -1 to 1
- phase: float32 [131072], P('feat'), may hold values from 0 to 6.2832
- class_weights: float32 [131072, 147], P('feat'), may hold values from -40 to 40
- velocity: float32 [131072, 147], P('feat'), may hold values from -3 to 3
Outputs:
- weights_out: float32 [131072, 147], P('feat')
- velocity_out: float32 [131072, 147], P('feat')
The draws below stay inside these ranges and needn't reach their ends.
Inputs may be any that keep to these rules, and one draw needn't show every extreme that they name: labels come in runs of 4 to 12 consecutive frames that share one class (phone segments); neighbouring runs may share a class.
All inputs are finite; a program needn't handle non-finite values.
Results may differ from the reference program's by a relative error of at most 0.00011.
Values sent between devices are 32-bit elements; how exact they have to be, the bound alone decides.
A program may use at most 128 MiB of HBM per device.

```python
import math
import jax
import jax.numpy as jnp
from jax import lax

IN_DIM = 440
CLASSES = 147
FEAT_DEV = 2048
ITERS = 2
FEATS = 131072
FRAMES = 6144


def segment_layout(key):
    seg_slots = FRAMES // 4 + 1
    seg_len = jax.random.randint(jax.random.fold_in(key, 5), (seg_slots,), 4, 13)
    starts = jnp.cumsum(seg_len) - seg_len
    marks = jnp.zeros((FRAMES,), jnp.int32).at[starts].add(1, mode='drop')
    seg_ids = jnp.cumsum(marks) - 1
    seg_class = jax.random.randint(jax.random.fold_in(key, 6), (seg_slots,), 0, CLASSES)
    return (seg_slots, seg_ids, seg_class)


def base_arrays(key):
    seg_slots, seg_ids, seg_class = segment_layout(key)
    key_shared, key_own, key_proj, key_phase, key_width = jax.random.split(jax.random.fold_in(key, 11), 5)
    shared = jax.random.normal(key_shared, (seg_slots, IN_DIM), jnp.float32)
    own = jax.random.normal(key_own, (FRAMES, IN_DIM), jnp.float32)
    top_width = 2.5
    frames = 2.5 * (math.sqrt(0.9) * shared[seg_ids] + math.sqrt(0.1) * own)
    frames = jnp.clip(frames, -6.0, 6.0)
    block_count = FEATS // FEAT_DEV
    jitter = jax.random.uniform(key_width, (block_count,), jnp.float32, 0.0, 1.0)
    position = (jnp.arange(block_count, dtype=jnp.float32) + jitter) / block_count
    widths = jnp.exp((1.0 - position) * math.log(top_width))
    widths = jnp.repeat(widths, FEAT_DEV)
    proj = jnp.clip(jax.random.normal(key_proj, (IN_DIM, FEATS), jnp.float32), -6.0, 6.0) / math.sqrt(IN_DIM)
    proj = jnp.clip(proj * widths[None, :], -1.0, 1.0)
    phase = jax.random.uniform(key_phase, (FEATS,), jnp.float32, 0.0, 6.2832)
    return (frames, proj, phase)


def draw_frames(key, part):
    return base_arrays(key)[0]


def draw_labels(key, part):
    seg_slots, seg_ids, seg_class = segment_layout(key)
    return seg_class[seg_ids].astype(jnp.int32)


def draw_proj(key, part):
    return base_arrays(key)[1]


def draw_phase(key, part):
    return base_arrays(key)[2]


def draw_class_weights(key, part):
    weights = 3.0 * jnp.clip(jax.random.normal(jax.random.fold_in(key, 23), (FEATS, CLASSES), jnp.float32), -6.0, 6.0)
    return weights


def level_of(key, extent, pieces, least, top_value):
    gain, own = 1.0, jax.random.fold_in(key, 6)
    for dim, blocks in pieces:
        draws = jnp.exp(jax.random.uniform(jax.random.fold_in(own, dim), (blocks,), jnp.float32, least / len(pieces), top_value / len(pieces)))
        gain = gain * jnp.repeat(draws, extent[dim] // blocks).reshape([-1 if axis == dim else 1 for axis in range(len(extent))])
    return gain


def bell_draw(key, dims, width, most, cuts=(), kind=jnp.bfloat16):
    drawn = jax.random.normal(key, dims, jnp.float32) * width
    if len(cuts) > 0:
        drawn = level_of(key, dims, cuts, -0.22, 0.18) * drawn
    return jnp.clip(drawn, min=-most, max=most).astype(kind)


def setup_inputs(seed: int = 0) -> dict:
    seeds = jax.random.split(jax.random.key(seed), 7)
    frames = draw_frames(jax.random.fold_in(seeds[6], 71), 0)
    labels = draw_labels(jax.random.fold_in(seeds[6], 71), 0)
    proj = draw_proj(jax.random.fold_in(seeds[6], 71), 0)
    phase = draw_phase(jax.random.fold_in(seeds[6], 71), 0)
    class_weights = draw_class_weights(jax.random.fold_in(seeds[6], 71), 0)
    velocity = bell_draw(seeds[5], (FEATS, CLASSES), 0.5, 3.0, ((0, 64),), jnp.float32)
    return dict(frames=frames, labels=labels, proj=proj, phase=phase, class_weights=class_weights, velocity=velocity)


MOMENTUM = 0.9
STEP_RATE = 0.05
EPSILON = 1e-06

def featurize(frame_rows, proj_block, phase_block):
    angles = jnp.dot(frame_rows, proj_block, precision=lax.Precision.HIGHEST, preferred_element_type=jnp.float32)
    return math.sqrt(2.0 / FEATS) * jnp.cos(angles + phase_block[None, :])

def reference(frames, labels, proj, phase, class_weights, velocity):
    block_width = math.gcd(FEATS, 4096)
    block_count = FEATS // block_width
    onehot = (labels[:, None] == jnp.arange(CLASSES, dtype=jnp.int32)[None, :]).astype(jnp.float32)
    proj_blocks = proj.reshape(IN_DIM, block_count, block_width).transpose(1, 0, 2)
    phase_blocks = phase.reshape(block_count, block_width)
    weights_now = class_weights
    velocity_now = velocity
    for iteration in range(ITERS):
        advance = weights_now + MOMENTUM * velocity_now
        look_blocks = advance.reshape(block_count, block_width, CLASSES)

        def add_scores(scores, inputs_block):
            proj_block, phase_block, look_block = inputs_block
            features = featurize(frames, proj_block, phase_block)
            return (scores + jnp.dot(features, look_block, precision=lax.Precision.HIGHEST, preferred_element_type=jnp.float32), None)
        scores, unused = lax.scan(add_scores, jnp.zeros((FRAMES, CLASSES), jnp.float32), (proj_blocks, phase_blocks, look_blocks))
        row_max = lax.optimization_barrier(jnp.max(scores, axis=1, keepdims=True))
        exponent = jnp.exp(scores - row_max)
        probability = exponent / lax.optimization_barrier(jnp.sum(exponent, axis=1, keepdims=True))
        residual = probability - onehot

        def grad_block(inputs_block):
            proj_block, phase_block = inputs_block
            features = featurize(frames, proj_block, phase_block)
            return lax.dot_general(features, residual, (((0,), (0,)), ((), ())), precision=lax.Precision.HIGHEST, preferred_element_type=jnp.float32)
        gradient = lax.map(grad_block, (proj_blocks, phase_blocks)).reshape(FEATS, CLASSES)
        grad_rms = jnp.sqrt(jnp.sum(gradient * gradient) / (FEATS * CLASSES) + EPSILON)
        velocity_now = MOMENTUM * velocity_now - STEP_RATE * gradient / grad_rms
        weights_now = weights_now + velocity_now
    return (weights_now, velocity_now)
```

```python
import functools
import math

import jax
import jax.numpy as jnp
from jax import lax
from jax.experimental import pallas as pl
from jax.experimental.pallas import tpu as pltpu
from jax.sharding import PartitionSpec as P

MOMENTUM = 0.9
STEP_RATE = 0.05
EPSILON = 1e-06
TURN = 1.0 / (2.0 * math.pi)
ROUNDER = 1.5 * 2.0**23
SINE = (
    6.283185160089458,
    -41.34165503141172,
    81.60100407300267,
    -76.54978228814288,
    39.53670602749812,
)
MESH = pl.DeviceIdType.MESH
VMEM_LIMIT = 60 * 2**20
CLASS_PAD = 160
UNIT = CLASS_PAD // 2


def positions():
    index = lax.axis_index("feat")
    return {"z": index // 16, "x": (index // 4) % 4, "y": index % 4}


def feat_at(pos, dim, step):
    moved = dict(pos)
    moved[dim] = (pos[dim] + step) % 4
    return moved["z"] * 16 + moved["x"] * 4 + moved["y"]


class Copies:
    def __init__(self, send_sems, recv_sems):
        self.send_sems, self.recv_sems, self.made = send_sems, recv_sems, []

    def send(self, src, dst, device):
        slot = len(self.made)
        copy = pltpu.make_async_remote_copy(
            src_ref=src,
            dst_ref=dst,
            send_sem=self.send_sems.at[slot],
            recv_sem=self.recv_sems.at[slot],
            device_id=device,
            device_id_type=MESH,
        )
        copy.start()
        self.made.append(copy)
        return copy

    def wait_sends(self):
        for copy in self.made:
            copy.wait_send()


def greet(devices):
    barrier = pltpu.get_barrier_semaphore()
    for device in devices:
        pl.semaphore_signal(barrier, inc=1, device_id=device, device_id_type=MESH)
    pl.semaphore_wait(barrier, len(devices))


def gather_ring(copies, pos, dim, source, block):
    here = pos[dim]
    right = {"feat": feat_at(pos, dim, 1)}
    left = {"feat": feat_at(pos, dim, 3)}
    before, after = (here + 3) % 4, (here + 1) % 4
    first_right = copies.send(source(0), block(here, 0), right)
    first_left = copies.send(source(1), block(here, 1), left)
    second_right = copies.send(source(1), block(here, 1), right)
    second_left = copies.send(source(0), block(here, 0), left)
    yield
    first_right.wait_recv()
    on_right = copies.send(block(before, 0), block(before, 0), right)
    first_left.wait_recv()
    on_left = copies.send(block(after, 1), block(after, 1), left)
    yield
    for copy in (second_right, second_left, on_right, on_left):
        copy.wait_recv()


def run_all(streams):
    streams = list(streams)
    while streams:
        alive = []
        for stream in streams:
            try:
                next(stream)
                alive.append(stream)
            except StopIteration:
                pass
        streams = alive


COLOURS = (("y", "x", "z"), ("x", "z", "y"), ("z", "y", "x"))
FRAME_COPIES = 3 * 3 * 6
SCORE_COPIES = 3 * (6 + 6 + 3 + 6 + 6)


def frames_kernel(x_ref, out_ref, send_sems, recv_sems, local_sem):
    pos = positions()
    greet([{"feat": feat_at(pos, dim, step)} for dim in "zxy" for step in (1, 3)])
    copies = Copies(send_sems, recv_sems)
    own = pltpu.make_async_copy(x_ref, out_ref.at[pos["z"], pos["x"], pos["y"]], local_sem)
    own.start()
    state = {"own": False}
    third = x_ref.shape[0] // 3
    half = third // 2

    def colour(c, dims):
        done = []
        for dim in dims:

            def block(q, h, dim=dim, done=tuple(done)):
                index = tuple(
                    slice(None) if name in done else (q if name == dim else pos[name])
                    for name in "zxy"
                )
                return out_ref.at[index + (pl.ds(third * c + half * h, half),)]

            def source(h, block=block, dim=dim, first=not done):
                if first:
                    return x_ref.at[pl.ds(third * c + half * h, half)]
                return block(pos[dim], h)

            yield from gather_ring(copies, pos, dim, source, block)
            if not state["own"]:
                own.wait()
                state["own"] = True
            done.append(dim)
            yield

    run_all([colour(c, dims) for c, dims in enumerate(COLOURS)])
    copies.wait_sends()


def gather_frames(frames):
    rows, width = frames.shape
    return pl.pallas_call(
        frames_kernel,
        out_shape=jax.ShapeDtypeStruct((4, 4, 4, rows, width), jnp.float32),
        in_specs=[pl.BlockSpec(memory_space=pl.ANY)],
        out_specs=pl.BlockSpec(memory_space=pl.ANY),
        scratch_shapes=[
            pltpu.SemaphoreType.DMA((FRAME_COPIES,)),
            pltpu.SemaphoreType.DMA((FRAME_COPIES,)),
            pltpu.SemaphoreType.DMA,
        ],
        compiler_params=pltpu.CompilerParams(collective_id=0, has_side_effects=True),
        name="gather_frames",
    )(frames)


def scores_kernel(
    p_ref, out_ref, total, from_left, from_right, onward_r, onward_l, sum_left, sum_right, kept,
    small_left, small_right, small_r, small_l, unit_left, unit_right, unit, others,
    send_sems, recv_sems,
):
    pos = positions()
    greet([{"feat": feat_at(pos, dim, step)} for dim in "zxy" for step in (1, 2, 3)])
    copies = Copies(send_sems, recv_sems)
    half = UNIT // 2

    def colour(c, dims):
        d1, d2, d3 = dims
        a, b = pos[d1], pos[d2]
        base = 16 * c

        def part(i, h):
            return pl.ds(base + 4 * i + 2 * h, 2)

        right, left = {"feat": feat_at(pos, d1, 1)}, {"feat": feat_at(pos, d1, 3)}
        far, after, before = (a + 2) % 4, (a + 1) % 4, (a + 3) % 4
        s1 = copies.send(p_ref.at[part(far, 0)], from_left.at[c], right)
        s2 = copies.send(p_ref.at[part(far, 1)], from_right.at[c], left)
        s3 = copies.send(p_ref.at[part(after, 1)], sum_left.at[c, 1], right)
        s4 = copies.send(p_ref.at[part(before, 0)], sum_right.at[c, 0], left)
        yield
        s1.wait_recv()
        onward_r[c] = p_ref[part(after, 0)] + from_left[c]
        s5 = copies.send(onward_r.at[c], sum_left.at[c, 0], right)
        s2.wait_recv()
        onward_l[c] = p_ref[part(before, 1)] + from_right[c]
        s6 = copies.send(onward_l.at[c], sum_right.at[c, 1], left)
        yield
        for copy in (s3, s4, s5, s6):
            copy.wait_recv()
        for h in range(2):
            kept[c, pl.ds(2 * h, 2)] = p_ref[part(a, h)] + (sum_left[c, h] + sum_right[c, h])

        right, left = {"feat": feat_at(pos, d2, 1)}, {"feat": feat_at(pos, d2, 3)}
        far, after, before = (b + 2) % 4, (b + 1) % 4, (b + 3) % 4
        low, high = pl.ds(0, half), pl.ds(half, half)
        s1 = copies.send(kept.at[c, far, low], small_left.at[c], right)
        s2 = copies.send(kept.at[c, far, high], small_right.at[c], left)
        s3 = copies.send(kept.at[c, after, high], unit_left.at[c, 1], right)
        s4 = copies.send(kept.at[c, before, low], unit_right.at[c, 0], left)
        yield
        s1.wait_recv()
        small_r[c] = kept[c, after, low] + small_left[c]
        s5 = copies.send(small_r.at[c], unit_left.at[c, 0], right)
        s2.wait_recv()
        small_l[c] = kept[c, before, high] + small_right[c]
        s6 = copies.send(small_l.at[c], unit_right.at[c, 1], left)
        yield
        for copy in (s3, s4, s5, s6):
            copy.wait_recv()
        for h, rows in enumerate((low, high)):
            unit[c, rows] = kept[c, b, rows] + (unit_left[c, h] + unit_right[c, h])

        parts = [
            copies.send(unit.at[c], others.at[c, slot], {"feat": feat_at(pos, d3, step)})
            for slot, step in enumerate((2, 1, 3))
        ]
        yield
        for copy in parts:
            copy.wait_recv()
        total[base + 4 * a + b] = (unit[c] + others[c, 0]) + (others[c, 1] + others[c, 2])

        def unit_block(q, h):
            return total.at[base + 4 * a + q, pl.ds(half * h, half)]

        yield from gather_ring(copies, pos, d2, lambda h: unit_block(b, h), unit_block)

        def row_block(q, h):
            return total.at[part(q, h)]

        yield from gather_ring(copies, pos, d1, lambda h: row_block(a, h), row_block)

    run_all([colour(c, dims) for c, dims in enumerate(COLOURS)])

    def put(u, carry):
        out_ref[u] = total[u]
        return carry

    lax.fori_loop(0, total.shape[0], put, 0)
    copies.wait_sends()


def sum_scores(partial_scores, collective_id):
    units = partial_scores.shape[0]
    f32 = jnp.float32
    half = UNIT // 2
    return pl.pallas_call(
        scores_kernel,
        out_shape=jax.ShapeDtypeStruct(partial_scores.shape, f32),
        in_specs=[pl.BlockSpec(memory_space=pltpu.VMEM)],
        out_specs=pl.BlockSpec(memory_space=pltpu.VMEM),
        scratch_shapes=[
            pltpu.VMEM((units, UNIT, 128), f32),
            pltpu.VMEM((3, 2, UNIT, 128), f32),
            pltpu.VMEM((3, 2, UNIT, 128), f32),
            pltpu.VMEM((3, 2, UNIT, 128), f32),
            pltpu.VMEM((3, 2, UNIT, 128), f32),
            pltpu.VMEM((3, 2, 2, UNIT, 128), f32),
            pltpu.VMEM((3, 2, 2, UNIT, 128), f32),
            pltpu.VMEM((3, 4, UNIT, 128), f32),
            pltpu.VMEM((3, half, 128), f32),
            pltpu.VMEM((3, half, 128), f32),
            pltpu.VMEM((3, half, 128), f32),
            pltpu.VMEM((3, half, 128), f32),
            pltpu.VMEM((3, 2, half, 128), f32),
            pltpu.VMEM((3, 2, half, 128), f32),
            pltpu.VMEM((3, UNIT, 128), f32),
            pltpu.VMEM((3, 3, UNIT, 128), f32),
            pltpu.SemaphoreType.DMA((SCORE_COPIES,)),
            pltpu.SemaphoreType.DMA((SCORE_COPIES,)),
        ],
        compiler_params=pltpu.CompilerParams(
            collective_id=collective_id, has_side_effects=True, vmem_limit_bytes=VMEM_LIMIT
        ),
        name=f"sum_scores_{collective_id}",
    )(partial_scores)


def split(value):
    high = value.astype(jnp.bfloat16)
    return high, (value - high.astype(jnp.float32)).astype(jnp.bfloat16)


def mul(left, right):
    return jnp.dot(left, right, preferred_element_type=jnp.float32)


def load_advance(w_ref, v_ref, a_high, a_low, scale):
    classes = w_ref.shape[1]
    a_high[...] = jnp.zeros_like(a_high)
    a_low[...] = jnp.zeros_like(a_low)
    rows = 256

    def part(i, carry):
        at = pl.ds(pl.multiple_of(i * rows, rows), rows)
        high, low = split((w_ref[at, :] + MOMENTUM * v_ref[at, :]) * scale)
        a_high[at, :classes] = high
        a_low[at, :classes] = low
        return carry

    lax.fori_loop(0, w_ref.shape[0] // rows, part, 0)


def put_scores(out_ref, scores):
    flipped = scores.T
    for k in range(scores.shape[0] // 128):
        out_ref[k] = flipped[:CLASS_PAD, 128 * k : 128 * (k + 1)]


def features_kernel(
    scale, x_ref, proj_ref, phase_ref, w_ref, v_ref, high_ref, low_ref, out_ref,
    x_pad, proj_pad, p_high, p_low, a_high, a_low,
):
    depth = x_ref.shape[1]
    padded = x_pad.shape[1]
    width = proj_ref.shape[1]

    @pl.when(pl.program_id(0) == 0)
    def _():
        load_advance(w_ref, v_ref, a_high, a_low, scale)
        proj_pad[...] = jnp.zeros_like(proj_pad)
        proj_pad[:depth, :] = proj_ref[...] * TURN
        phase = phase_ref[...] * TURN
        top = phase.astype(jnp.bfloat16).astype(jnp.float32)
        row = lax.broadcasted_iota(jnp.int32, (8, width), 0)
        proj_pad[depth : depth + 8, :] = jnp.where(
            row == 0, top, jnp.where(row == 1, phase - top, 0.0)
        )
        step = 64
        for k in range(padded // step):
            at = pl.ds(k * step, step)
            p_high[at, :], p_low[at, :] = split(proj_pad[at, :])
        lane = lax.broadcasted_iota(jnp.int32, x_pad.shape, 1)
        x_pad[...] = jnp.where((lane == depth) | (lane == depth + 1), 1.0, 0.0)

    x_pad[:, :depth] = x_ref[...]
    x_high, x_low = split(x_pad[...])
    tile = 256
    for n in range(width // tile):
        at = pl.ds(n * tile, tile)
        turns = mul(x_high, p_high[:, at]) + mul(x_high, p_low[:, at]) + mul(x_low, p_high[:, at])
        turns = turns - ((turns + ROUNDER) - ROUNDER)
        quarter = 0.25 - jnp.abs(turns)
        square = quarter * quarter
        value = SINE[4]
        for coefficient in SINE[3::-1]:
            value = value * square + coefficient
        high_ref[:, at], low_ref[:, at] = split(value * quarter)
    high, low = high_ref[...], low_ref[...]
    put_scores(
        out_ref, mul(high, a_high[...]) + mul(high, a_low[...]) + mul(low, a_high[...])
    )


def make_features(frames, proj, phase, weights, velocity, scale):
    count, depth = frames.shape
    width, classes = weights.shape
    block = 256
    padded = 512
    bf16 = jnp.bfloat16
    whole = lambda shape: pl.BlockSpec(shape, lambda i: (0, 0), pipeline_mode=pl.Buffered(1))
    return pl.pallas_call(
        functools.partial(features_kernel, scale),
        grid=(count // block,),
        out_shape=[
            jax.ShapeDtypeStruct((count, width), bf16),
            jax.ShapeDtypeStruct((count, width), bf16),
            jax.ShapeDtypeStruct((count // 128, CLASS_PAD, 128), jnp.float32),
        ],
        in_specs=[
            pl.BlockSpec((block, depth), lambda i: (i, 0)),
            whole((depth, width)),
            whole((1, width)),
            whole((width, classes)),
            whole((width, classes)),
        ],
        out_specs=[
            pl.BlockSpec((block, width), lambda i: (i, 0)),
            pl.BlockSpec((block, width), lambda i: (i, 0)),
            pl.BlockSpec((block // 128, CLASS_PAD, 128), lambda i: (i, 0, 0)),
        ],
        scratch_shapes=[
            pltpu.VMEM((block, padded), jnp.float32),
            pltpu.VMEM((padded, width), jnp.float32),
            pltpu.VMEM((padded, width), bf16),
            pltpu.VMEM((padded, width), bf16),
            pltpu.VMEM((width, 256), bf16),
            pltpu.VMEM((width, 256), bf16),
        ],
        compiler_params=pltpu.CompilerParams(vmem_limit_bytes=VMEM_LIMIT),
        name="make_features",
    )(frames, proj, phase.reshape(1, width), weights, velocity)


def rescore_kernel(scale, high_ref, low_ref, w_ref, v_ref, out_ref, a_high, a_low):
    @pl.when(pl.program_id(0) == 0)
    def _():
        load_advance(w_ref, v_ref, a_high, a_low, scale)

    high, low = high_ref[...], low_ref[...]
    put_scores(
        out_ref, mul(high, a_high[...]) + mul(high, a_low[...]) + mul(low, a_high[...])
    )


def rescore(high, low, weights, velocity, scale):
    count, width = high.shape
    classes = weights.shape[1]
    block = 512
    whole = lambda shape: pl.BlockSpec(shape, lambda i: (0, 0), pipeline_mode=pl.Buffered(1))
    return pl.pallas_call(
        functools.partial(rescore_kernel, scale),
        grid=(count // block,),
        out_shape=jax.ShapeDtypeStruct((count // 128, CLASS_PAD, 128), jnp.float32),
        in_specs=[
            pl.BlockSpec((block, width), lambda i: (i, 0)),
            pl.BlockSpec((block, width), lambda i: (i, 0)),
            whole((width, classes)),
            whole((width, classes)),
        ],
        out_specs=pl.BlockSpec((block // 128, CLASS_PAD, 128), lambda i: (i, 0, 0)),
        scratch_shapes=[
            pltpu.VMEM((width, 256), jnp.bfloat16),
            pltpu.VMEM((width, 256), jnp.bfloat16),
        ],
        compiler_params=pltpu.CompilerParams(vmem_limit_bytes=VMEM_LIMIT),
        name="rescore",
    )(high, low, weights, velocity)


def gradient_kernel(scale, classes, scores_ref, labels_ref, high_ref, low_ref, out_ref, stack):
    groups = scores_ref.shape[0]
    step = pl.program_id(0)
    row = lax.broadcasted_iota(jnp.int32, (CLASS_PAD, 128), 0)
    for k in range(groups):
        scores = jnp.where(row < classes, scores_ref[k], -jnp.inf)
        exponent = jnp.exp(scores - jnp.max(scores, axis=0, keepdims=True))
        probability = exponent / jnp.sum(exponent, axis=0, keepdims=True)
        label = labels_ref[pl.ds(step * groups + k, 1), :]
        residual = (probability - jnp.where(row == label, 1.0, 0.0)) * scale
        at = pl.ds(128 * k, 128)
        stack[:CLASS_PAD, at], stack[CLASS_PAD:, at] = split(residual)
    both = mul(stack[...], high_ref[...])
    value = both[:CLASS_PAD] + both[CLASS_PAD:] + mul(stack[:CLASS_PAD, :], low_ref[...])

    @pl.when(step == 0)
    def _():
        out_ref[...] = value

    @pl.when(step > 0)
    def _():
        out_ref[...] += value


def make_gradient(scores, labels, high, low, scale, classes):
    count, width = high.shape
    block = 512
    groups = block // 128
    return pl.pallas_call(
        functools.partial(gradient_kernel, scale, classes),
        grid=(count // block,),
        out_shape=jax.ShapeDtypeStruct((CLASS_PAD, width), jnp.float32),
        in_specs=[
            pl.BlockSpec((groups, CLASS_PAD, 128), lambda i: (i, 0, 0)),
            pl.BlockSpec((count // 128, 128), lambda i: (0, 0), pipeline_mode=pl.Buffered(1)),
            pl.BlockSpec((block, width), lambda i: (i, 0)),
            pl.BlockSpec((block, width), lambda i: (i, 0)),
        ],
        out_specs=pl.BlockSpec((CLASS_PAD, width), lambda i: (0, 0)),
        scratch_shapes=[pltpu.VMEM((2 * CLASS_PAD, block), jnp.bfloat16)],
        compiler_params=pltpu.CompilerParams(vmem_limit_bytes=VMEM_LIMIT),
        name="make_gradient",
    )(scores, labels, high, low)


def update_kernel(
    count_all, g_ref, w_ref, v_ref, w_out, v_out, other, squares, others, send_sems, recv_sems
):
    pos = positions()
    partner = {"frame": 1 - lax.axis_index("frame")}
    greet(
        [partner]
        + [{"feat": feat_at(pos, dim, step)} for dim in "zxy" for step in (1, 2, 3)]
    )
    copies = Copies(send_sems, recv_sems)
    classes = w_ref.shape[1]
    width = g_ref.shape[1]
    copies.send(g_ref, other, partner).wait_recv()

    def square(j, total):
        at = pl.ds(pl.multiple_of(j * 128, 128), 128)
        value = g_ref[:, at] + other[:, at]
        value = value * value
        return total + jnp.sum(value.reshape(CLASS_PAD // 8, 8, 128), axis=0)

    squares[0] = lax.fori_loop(0, width // 128, square, jnp.zeros((8, 128), jnp.float32))
    for stage, dim in enumerate("zxy"):
        parts = [
            copies.send(
                squares.at[stage], others.at[stage, slot], {"feat": feat_at(pos, dim, step)}
            )
            for slot, step in enumerate((2, 1, 3))
        ]
        for copy in parts:
            copy.wait_recv()
        squares[stage + 1] = (squares[stage] + others[stage, 0]) + (
            others[stage, 1] + others[stage, 2]
        )
    square_sum = jnp.sum(squares[3], axis=(0, 1), keepdims=True)
    rate = STEP_RATE / jnp.sqrt(square_sum / count_all + EPSILON)

    def update(j, carry):
        at = pl.ds(pl.multiple_of(j * 128, 128), 128)
        flipped = (g_ref[:, at] + other[:, at]).T
        speed = MOMENTUM * v_ref[at, :] - rate * flipped[:, :classes]
        v_out[at, :] = speed
        w_out[at, :] = w_ref[at, :] + speed
        return carry

    lax.fori_loop(0, width // 128, update, 0)
    copies.wait_sends()


def update(gradient, weights, velocity, count_all, collective_id):
    f32 = jnp.float32
    shape = jax.ShapeDtypeStruct(weights.shape, f32)
    vmem = pl.BlockSpec(memory_space=pltpu.VMEM)
    return pl.pallas_call(
        functools.partial(update_kernel, count_all),
        out_shape=[shape, shape],
        in_specs=[vmem] * 3,
        out_specs=[vmem] * 2,
        scratch_shapes=[
            pltpu.VMEM(gradient.shape, f32),
            pltpu.VMEM((4, 8, 128), f32),
            pltpu.VMEM((3, 3, 8, 128), f32),
            pltpu.SemaphoreType.DMA((10,)),
            pltpu.SemaphoreType.DMA((10,)),
        ],
        compiler_params=pltpu.CompilerParams(
            collective_id=collective_id, has_side_effects=True, vmem_limit_bytes=VMEM_LIMIT
        ),
        name=f"update_{collective_id}",
    )(gradient, weights, velocity)


def on_device(frames, labels, proj, phase, class_weights, velocity):
    feat_count = 64 * proj.shape[1]
    classes = class_weights.shape[1]
    scale = math.sqrt(2.0 / feat_count)
    count_all = feat_count * classes
    count = labels.shape[0]
    labels = labels.reshape(count // 128, 128)
    everyone = gather_frames(frames).reshape(count, frames.shape[1])
    high, low, partial = make_features(everyone, proj, phase, class_weights, velocity, scale)
    units = (count // 64, UNIT, 128)
    for iteration in range(2):
        if iteration:
            partial = rescore(high, low, class_weights, velocity, scale)
        scores = sum_scores(partial.reshape(units), 1 + 2 * iteration).reshape(partial.shape)
        gradient = make_gradient(scores, labels, high, low, scale, classes)
        class_weights, velocity = update(
            gradient, class_weights, velocity, count_all, 2 + 2 * iteration
        )
    return class_weights, velocity


def solution(mesh):
    return jax.shard_map(
        on_device,
        mesh=mesh,
        in_specs=(
            P(("frame", "feat"), None),
            P("frame"),
            P(None, "feat"),
            P("feat"),
            P("feat", None),
            P("feat", None),
        ),
        out_specs=(P("feat", None), P("feat", None)),
        check_vma=False,
    )
```

```python
import functools
import math

import jax
import jax.numpy as jnp
from jax import lax
from jax.experimental import pallas as pl
from jax.experimental.pallas import tpu as pltpu
from jax.sharding import PartitionSpec as P

MOMENTUM = 0.9
STEP_RATE = 0.05
EPSILON = 1e-06
ITERS = 2
TURN = 1.0 / (2.0 * math.pi)
ROUNDER = 1.5 * 2.0**23
SINE = (
    6.283185160089458,
    -41.34165503141172,
    81.60100407300267,
    -76.54978228814288,
    39.53670602749812,
)
MESH = pl.DeviceIdType.MESH
VMEM_LIMIT = 67043328
CLASS_PAD = 160
UNIT = 40
COLOURS = (("y", "x", "z"), ("x", "z", "y"), ("z", "y", "x"))
FRAME_COPIES = 3 * 3 * 6
CHUNKS = 2
SCORE_COPIES = CHUNKS * 3 * (3 + 3 + 3 + 3 + 6)
SQUARE_COPIES = 9
TILE = 512


def positions():
    index = lax.axis_index("feat")
    return {"z": index // 16, "x": (index // 4) % 4, "y": index % 4}


class Copies:
    def __init__(self, pos, send_sems, recv_sems, first):
        self.pos, self.send_sems, self.recv_sems = pos, send_sems, recv_sems
        self.first, self.made = first, []

    def device(self, dim, step):
        moved = dict(self.pos)
        moved[dim] = (self.pos[dim] + step) % 4
        return {"feat": moved["z"] * 16 + moved["x"] * 4 + moved["y"]}

    def make(self, src, dst, dim, step):
        slot = self.first + len(self.made)
        copy = pltpu.make_async_remote_copy(
            src_ref=src,
            dst_ref=dst,
            send_sem=self.send_sems.at[slot],
            recv_sem=self.recv_sems.at[slot],
            device_id=self.device(dim, step),
            device_id_type=MESH,
        )
        self.made.append(copy)
        return copy

    def send(self, src, dst, dim, step):
        copy = self.make(src, dst, dim, step)
        copy.start()
        return copy

    def wait_sends(self):
        for copy in self.made:
            copy.wait_send()


def ring_copies(copies, dim, source, block):
    here = copies.pos[dim]
    before, after = (here + 3) % 4, (here + 1) % 4
    return (
        copies.make(source(0), block(here, 0), dim, 1),
        copies.make(source(1), block(here, 1), dim, 3),
        copies.make(source(1), block(here, 1), dim, 1),
        copies.make(source(0), block(here, 0), dim, 3),
        copies.make(block(before, 0), block(before, 0), dim, 1),
        copies.make(block(after, 1), block(after, 1), dim, 3),
    )


def gather_ring(copies, dim, source, block):
    ring = ring_copies(copies, dim, source, block)
    for copy in ring[:4]:
        copy.start()
    yield
    ring[0].wait_recv()
    ring[4].start()
    ring[1].wait_recv()
    ring[5].start()
    yield
    for copy in ring[2:]:
        copy.wait_recv()


def advance_all(streams):
    alive = []
    for stream in streams:
        try:
            next(stream)
            alive.append(stream)
        except StopIteration:
            pass
    return alive


def split(value):
    high = value.astype(jnp.bfloat16)
    return high, (value - high.astype(jnp.float32)).astype(jnp.bfloat16)


def mul(left, right):
    return jnp.dot(left, right, preferred_element_type=jnp.float32)


def mul_flipped(left, right):
    return lax.dot_general(
        left, right, (((1,), (1,)), ((), ())), preferred_element_type=jnp.float32
    )


def sum_chunk(copies, chunk, colour, p_ref, total, wide, kept, narrow, unit, others):
    d1, d2, d3 = COLOURS[colour]
    pos = copies.pos
    a, b = pos[d1], pos[d2]
    base = 48 * chunk + 16 * colour
    c = 3 * chunk + colour
    steps = (2, 1, 3)

    def row(i):
        return pl.ds(base + 4 * i, 4)

    sent = [
        copies.send(p_ref.at[row((a + step) % 4)], wide.at[c, slot], d1, step)
        for slot, step in enumerate(steps)
    ]
    yield
    for copy in sent:
        copy.wait_recv()
    kept[c] = (p_ref[row(a)] + wide[c, 0]) + (wide[c, 1] + wide[c, 2])
    sent = [
        copies.send(kept.at[c, (b + step) % 4], narrow.at[c, slot], d2, step)
        for slot, step in enumerate(steps)
    ]
    yield
    for copy in sent:
        copy.wait_recv()
    unit[c] = (kept[c, b] + narrow[c, 0]) + (narrow[c, 1] + narrow[c, 2])
    sent = [
        copies.send(unit.at[c], others.at[c, slot], d3, step) for slot, step in enumerate(steps)
    ]
    yield
    for copy in sent:
        copy.wait_recv()
    mine = base + 4 * a + b
    total[mine] = (unit[c] + others[c, 0]) + (others[c, 1] + others[c, 2])
    sent = [copies.send(total.at[mine], total.at[mine], d2, step) for step in steps]
    yield
    for copy in sent:
        copy.wait_recv()

    def block(q, h):
        return total.at[pl.ds(base + 4 * q + 2 * h, 2)]

    yield from gather_ring(copies, d1, lambda h: block(a, h), block)


def kernel(
    scale, count_all, x_hbm, labels_ref, proj_hbm, phase_ref, w_hbm, v_hbm, w_ref, v_ref,
    everyone, proj_ref, p_high, p_low, x_pad, f_high, f_low, a_stack, p_ref, total,
    wide, kept, narrow, unit, others, r_stack, g_ref, g_other, squares, square_parts,
    send_sems, recv_sems, pair_send, pair_recv, load_sems,
):
    pos = positions()
    classes, width = w_ref.shape
    depth = x_hbm.shape[1]
    frames = f_high.shape[0]
    partner = {"frame": 1 - lax.axis_index("frame")}
    own_x = pltpu.make_async_copy(
        x_hbm, everyone.at[pos["z"], pos["x"], pos["y"]], load_sems.at[0]
    )
    load_proj = pltpu.make_async_copy(proj_hbm, proj_ref, load_sems.at[1])
    load_w = pltpu.make_async_copy(w_hbm, w_ref, load_sems.at[2])
    load_v = pltpu.make_async_copy(v_hbm, v_ref, load_sems.at[3])
    for load in (own_x, load_proj, load_w, load_v):
        load.start()

    copies = Copies(pos, send_sems, recv_sems, 0)
    barrier = pltpu.get_barrier_semaphore()
    peers = [partner] + [copies.device(dim, step) for dim in "zxy" for step in (1, 2, 3)]
    for peer in peers:
        pl.semaphore_signal(barrier, inc=1, device_id=peer, device_id_type=MESH)
    pl.semaphore_wait(barrier, len(peers))

    def piece(dims, colour, done, q, h):
        at = tuple(
            slice(None) if name in done else (q if name == dims[len(done)] else pos[name])
            for name in "zxy"
        )
        return everyone.at[at + (pl.ds(16 * colour + 8 * h, 8),)]

    def near(colour):
        dims = COLOURS[colour]
        for count in range(2):
            block = functools.partial(piece, dims, colour, dims[:count])
            if count == 0:
                source = lambda h: x_hbm.at[pl.ds(16 * colour + 8 * h, 8)]
            else:
                source = functools.partial(block, pos[dims[1]])
            yield from gather_ring(copies, dims[count], source, block)
            if count == 0 and colour == 0:
                own_x.wait()

    def prepare_proj():
        load_proj.wait()
        whole = depth // 16 * 16
        step = 48
        for k in range(whole // step):
            at = pl.ds(k * step, step)
            p_high[at, :], p_low[at, :] = split(proj_ref[at, :] * TURN)
        phase = phase_ref[...] * TURN
        top = phase.astype(jnp.bfloat16).astype(jnp.float32)
        row = lax.broadcasted_iota(jnp.int32, (8, width), 0)
        tail = jnp.where(row == 0, top, jnp.where(row == 1, phase - top, 0.0))
        last = jnp.concatenate([proj_ref[whole:depth, :] * TURN, tail], axis=0)
        p_high[whole : whole + 16, :], p_low[whole : whole + 16, :] = split(last)
        rest = p_high.shape[0] - whole - 16
        p_high[whole + 16 :, :] = jnp.zeros((rest, width), jnp.bfloat16)
        p_low[whole + 16 :, :] = jnp.zeros((rest, width), jnp.bfloat16)

    def prepare_rest():
        lane = lax.broadcasted_iota(jnp.int32, x_pad.shape, 1)
        x_pad[...] = jnp.where((lane == depth) | (lane == depth + 1), 1.0, 0.0)
        a_stack[...] = jnp.zeros_like(a_stack)
        load_w.wait()
        load_v.wait()

    streams = advance_all([near(colour) for colour in range(3)])
    prepare_proj()
    streams = advance_all(streams)
    prepare_rest()
    while streams:
        streams = advance_all(streams)

    far = []
    for colour, dims in enumerate(COLOURS):
        block = functools.partial(piece, dims, colour, dims[:2])
        far.append(ring_copies(copies, dims[2], functools.partial(block, pos[dims[2]]), block))
    for slot in range(4):
        for ring in far:
            ring[slot].start()

    def features(i, carry):
        def when_arrived(step, slots):
            @pl.when(i == step)
            def _():
                for slot in slots:
                    for ring in far:
                        ring[slot].wait_recv()
                        if slot < 2:
                            ring[slot + 4].start()

        when_arrived(1, (0, 1))
        for slot in range(2, 6):
            when_arrived(slot + 2, (slot,))
        h = jnp.where((i == 1) | (i == 3) | (i == 4) | (i == 7), 1, 0)
        off = jnp.where(i < 2, 0, jnp.where(i > 5, 2, jnp.where((i == 2) | (i == 4), 3, 1)))
        rows = []
        for colour, dims in enumerate(COLOURS):
            q = (pos[dims[2]] + off) % 4
            at = tuple(q if name == dims[2] else slice(None) for name in "zxy")
            lines = pl.ds(pl.multiple_of(16 * colour + 8 * h, 8), 8)
            part = everyone[at + (lines, slice(None))]
            x_pad[128 * colour : 128 * (colour + 1), :depth] = part.reshape(128, depth)
            rows.append(pl.ds(pl.multiple_of(128 * (8 * colour + 4 * h + q), 128), 128))
        count = x_pad.shape[0]
        high, low = split(x_pad[...])
        both = jnp.concatenate([high, low], axis=0)
        step = 256
        for n in range(width // step):
            at = pl.ds(n * step, step)
            turns = mul(both, p_high[:, at])
            turns = turns[:count] + turns[count:] + mul(high, p_low[:, at])
            turns = turns - ((turns + ROUNDER) - ROUNDER)
            quarter = 0.25 - jnp.abs(turns)
            square = quarter * quarter
            value = SINE[4]
            for coefficient in SINE[3::-1]:
                value = value * square + coefficient
            top, bottom = split(value * quarter)
            for colour in range(3):
                f_high[rows[colour], at] = top[128 * colour : 128 * (colour + 1)]
                f_low[rows[colour], at] = bottom[128 * colour : 128 * (colour + 1)]
        return carry

    lax.fori_loop(0, 8, features, 0)
    copies.wait_sends()

    def exchange(iteration, n):
        return pltpu.make_async_remote_copy(
            src_ref=g_ref.at[n],
            dst_ref=g_other.at[iteration, n],
            send_sem=pair_send.at[n],
            recv_sem=pair_recv.at[iteration, n],
            device_id=partner,
            device_id_type=MESH,
        )

    tiles = width // TILE

    def optimize(iteration, carry):
        copies = Copies(pos, send_sems, recv_sems, FRAME_COPIES)

        def look_ahead(n, carry):
            at = pl.ds(pl.multiple_of(n * TILE, TILE), TILE)
            high, low = split((w_ref[:, at] + MOMENTUM * v_ref[:, at]) * scale)
            a_stack[:classes, at] = high
            a_stack[CLASS_PAD : CLASS_PAD + classes, at] = low
            return carry

        lax.fori_loop(0, tiles, look_ahead, 0)

        def score(n, carry):
            at = pl.ds(pl.multiple_of(n * TILE, TILE), TILE)
            both = mul_flipped(a_stack[...], f_high[at, :])
            low = mul_flipped(a_stack[:CLASS_PAD, :], f_low[at, :])
            scores = both[:CLASS_PAD] + both[CLASS_PAD:] + low
            for k in range(TILE // 128):
                part = scores[:, 128 * k : 128 * (k + 1)].reshape(4, UNIT, 128)
                p_ref[pl.ds(4 * (n * (TILE // 128) + k), 4)] = part
            return carry

        def residuals(block, carry):
            row = lax.broadcasted_iota(jnp.int32, (CLASS_PAD, 128), 0)
            scores = total[pl.ds(4 * block, 4)].reshape(CLASS_PAD, 128)
            scores = jnp.where(row < classes, scores, -jnp.inf)
            exponent = jnp.exp(scores - jnp.max(scores, axis=0, keepdims=True))
            probability = exponent / jnp.sum(exponent, axis=0, keepdims=True)
            label = labels_ref[pl.ds(block, 1), :]
            residual = (probability - jnp.where(row == label, 1.0, 0.0)) * scale
            at = pl.ds(pl.multiple_of(block * 128, 128), 128)
            r_stack[:CLASS_PAD, at], r_stack[CLASS_PAD:, at] = split(residual)
            return carry

        def gradient(chunk, n, carry):
            at = pl.ds(pl.multiple_of(n * TILE, TILE), TILE)
            rows = pl.ds(chunk * (frames // CHUNKS), frames // CHUNKS)
            both = mul(r_stack[:, rows], f_high[rows, at])
            value = both[:CLASS_PAD] + both[CLASS_PAD:]
            value = value + mul(r_stack[:CLASS_PAD, rows], f_low[rows, at])
            if chunk == 0:
                g_ref[n] = value
            else:
                g_ref[n] = g_ref[n] + value
            if chunk == CHUNKS - 1:
                exchange(iteration, n).start()
            return carry

        def streams(chunk):
            return [
                sum_chunk(
                    copies, chunk, colour, p_ref, total, wide, kept, narrow, unit, others
                )
                for colour in range(3)
            ]

        per_chunk = frames // TILE // CHUNKS
        lax.fori_loop(0, per_chunk, score, 0)
        early = advance_all(streams(0))
        lax.fori_loop(per_chunk, 2 * per_chunk, score, 0)
        late = advance_all(streams(1))
        while early:
            early = advance_all(early)
            if early:
                late = advance_all(late)
        blocks = frames // 128 // CHUNKS
        lax.fori_loop(0, blocks, residuals, 0)
        late = advance_all(late)
        lax.fori_loop(0, tiles, functools.partial(gradient, 0), 0)
        while late:
            late = advance_all(late)
        lax.fori_loop(blocks, 2 * blocks, residuals, 0)
        lax.fori_loop(0, tiles, functools.partial(gradient, 1), 0)

        summed = jnp.zeros((8, TILE), jnp.float32)
        for n in range(tiles):
            exchange(iteration, n).wait_recv()
            value = g_ref[n] + g_other[iteration, n]
            value = value * value
            summed = summed + jnp.sum(value.reshape(CLASS_PAD // 8, 8, TILE), axis=0)
        squares[0] = jnp.sum(
            jnp.stack([summed[:, 128 * k : 128 * (k + 1)] for k in range(TILE // 128)]), axis=0
        )
        for stage, dim in enumerate("zxy"):
            sent = [
                copies.send(squares.at[stage], square_parts.at[stage, slot], dim, step)
                for slot, step in enumerate((2, 1, 3))
            ]
            for copy in sent:
                copy.wait_recv()
            squares[stage + 1] = (squares[stage] + square_parts[stage, 0]) + (
                square_parts[stage, 1] + square_parts[stage, 2]
            )
        square_sum = jnp.sum(squares[3], axis=(0, 1), keepdims=True)
        rate = STEP_RATE / jnp.sqrt(square_sum / count_all + EPSILON)

        def update(n, carry):
            at = pl.ds(pl.multiple_of(n * TILE, TILE), TILE)
            value = g_ref[n, :classes] + g_other[iteration, n, :classes]
            speed = MOMENTUM * v_ref[:, at] - rate * value
            v_ref[:, at] = speed
            w_ref[:, at] = w_ref[:, at] + speed
            return carry

        lax.fori_loop(0, tiles, update, 0)
        copies.wait_sends()
        for n in range(tiles):
            exchange(iteration, n).wait_send()
        return carry

    lax.fori_loop(0, ITERS, optimize, 0)


def regroup(labels):
    parts = labels.reshape(4, 4, 4, 3, 2, 8)
    orders = ((3, 0, 1, 2, 4), (3, 2, 0, 1, 4), (3, 1, 0, 2, 4))
    return jnp.concatenate(
        [parts[:, :, :, c].transpose(order).reshape(8, 128) for c, order in enumerate(orders)]
    )


def on_device(frames, labels, proj, phase, class_weights, velocity):
    depth, width = proj.shape
    classes = class_weights.shape[1]
    feat_count = 64 * width
    scale = math.sqrt(2.0 / feat_count)
    count = labels.shape[0]
    f32, bf16 = jnp.float32, jnp.bfloat16
    units = count // 128 * 4
    colours = 3 * CHUNKS
    anywhere = pl.BlockSpec(memory_space=pl.ANY)
    vmem = pl.BlockSpec(memory_space=pltpu.VMEM)
    shape = jax.ShapeDtypeStruct((classes, width), f32)
    weights, speed = pl.pallas_call(
        functools.partial(kernel, scale, feat_count * classes),
        out_shape=[shape, shape],
        in_specs=[anywhere, vmem, anywhere, vmem, anywhere, anywhere],
        out_specs=[vmem, vmem],
        scratch_shapes=[
            pltpu.VMEM((4, 4, 4) + frames.shape, f32),
            pltpu.VMEM((depth, width), f32),
            pltpu.VMEM((512, width), bf16),
            pltpu.VMEM((512, width), bf16),
            pltpu.VMEM((384, 512), f32),
            pltpu.VMEM((count, width), bf16),
            pltpu.VMEM((count, width), bf16),
            pltpu.VMEM((2 * CLASS_PAD, width), bf16),
            pltpu.VMEM((units, UNIT, 128), f32),
            pltpu.VMEM((units, UNIT, 128), f32),
            pltpu.VMEM((colours, 3, 4, UNIT, 128), f32),
            pltpu.VMEM((colours, 4, UNIT, 128), f32),
            pltpu.VMEM((colours, 3, UNIT, 128), f32),
            pltpu.VMEM((colours, UNIT, 128), f32),
            pltpu.VMEM((colours, 3, UNIT, 128), f32),
            pltpu.VMEM((2 * CLASS_PAD, count), bf16),
            pltpu.VMEM((width // TILE, CLASS_PAD, TILE), f32),
            pltpu.VMEM((ITERS, width // TILE, CLASS_PAD, TILE), f32),
            pltpu.VMEM((4, 8, 128), f32),
            pltpu.VMEM((3, 3, 8, 128), f32),
            pltpu.SemaphoreType.DMA((FRAME_COPIES + SCORE_COPIES + SQUARE_COPIES,)),
            pltpu.SemaphoreType.DMA((FRAME_COPIES + SCORE_COPIES + SQUARE_COPIES,)),
            pltpu.SemaphoreType.DMA((width // TILE,)),
            pltpu.SemaphoreType.DMA((ITERS, width // TILE)),
            pltpu.SemaphoreType.DMA((4,)),
        ],
        compiler_params=pltpu.CompilerParams(
            collective_id=0, has_side_effects=True, vmem_limit_bytes=VMEM_LIMIT
        ),
        name="optimize",
    )(frames, regroup(labels), proj, phase.reshape(1, width), class_weights.T, velocity.T)
    return weights.T, speed.T


def solution(mesh):
    return jax.shard_map(
        on_device,
        mesh=mesh,
        in_specs=(
            P(("frame", "feat"), None),
            P("frame"),
            P(None, "feat"),
            P("feat"),
            P("feat", None),
            P("feat", None),
        ),
        out_specs=(P("feat", None), P("feat", None)),
        check_vma=False,
    )
```

```python
import functools
import math

import jax
import jax.numpy as jnp
from jax import lax
from jax.experimental import pallas as pl
from jax.experimental.pallas import tpu as pltpu
from jax.sharding import PartitionSpec as P

MOMENTUM = 0.9
STEP_RATE = 0.05
EPSILON = 1e-06
ITERS = 2
TURN = 1.0 / (2.0 * math.pi)
ROUNDER = 1.5 * 2.0**23
SINE = (
    6.283185160089458,
    -41.34165503141172,
    81.60100407300267,
    -76.54978228814288,
    39.53670602749812,
)
MESH = pl.DeviceIdType.MESH
VMEM_LIMIT = 67043328
CLASS_PAD = 160
UNIT = 40
COLOURS = (("y", "x", "z"), ("x", "z", "y"), ("z", "y", "x"))
FRAME_COPIES = 3 * (3 + 6 + 6)
CHUNKS = 2
SCORE_COPIES = CHUNKS * 3 * (3 + 3 + 3 + 3 + 6)
SQUARE_COPIES = 9
TILE = 512


def positions():
    index = lax.axis_index("feat")
    return {"z": index // 16, "x": (index // 4) % 4, "y": index % 4}


class Copies:
    def __init__(self, pos, send_sems, recv_sems, first):
        self.pos, self.send_sems, self.recv_sems = pos, send_sems, recv_sems
        self.slot, self.made = first, []

    def device(self, dim, step):
        moved = dict(self.pos)
        moved[dim] = (self.pos[dim] + step) % 4
        return {"feat": moved["z"] * 16 + moved["x"] * 4 + moved["y"]}

    def make(self, src, dst, dim, step):
        slot = self.slot
        self.slot += 1
        copy = pltpu.make_async_remote_copy(
            src_ref=src,
            dst_ref=dst,
            send_sem=self.send_sems.at[slot],
            recv_sem=self.recv_sems.at[slot],
            device_id=self.device(dim, step),
            device_id_type=MESH,
        )
        self.made.append(copy)
        return copy

    def send(self, src, dst, dim, step):
        copy = self.make(src, dst, dim, step)
        copy.start()
        return copy

    def wait_sends(self):
        for copy in self.made:
            copy.wait_send()
        self.made = []


def ring_copies(copies, dim, source, block):
    here = copies.pos[dim]
    before, after = (here + 3) % 4, (here + 1) % 4
    return (
        copies.make(source(0), block(here, 0), dim, 1),
        copies.make(source(1), block(here, 1), dim, 3),
        copies.make(source(1), block(here, 1), dim, 1),
        copies.make(source(0), block(here, 0), dim, 3),
        copies.make(block(before, 0), block(before, 0), dim, 1),
        copies.make(block(after, 1), block(after, 1), dim, 3),
    )


def gather_ring(copies, dim, source, block):
    ring = ring_copies(copies, dim, source, block)
    for copy in ring[:4]:
        copy.start()
    yield
    ring[0].wait_recv()
    ring[4].start()
    ring[1].wait_recv()
    ring[5].start()
    yield
    for copy in ring[2:]:
        copy.wait_recv()


def advance_all(streams):
    alive = []
    for stream in streams:
        try:
            next(stream)
            alive.append(stream)
        except StopIteration:
            pass
    return alive


def split(value):
    high = value.astype(jnp.bfloat16)
    return high, (value - high.astype(jnp.float32)).astype(jnp.bfloat16)


def mul(left, right):
    return jnp.dot(left, right, preferred_element_type=jnp.float32)


def mul_flipped(left, right):
    return lax.dot_general(
        left, right, (((1,), (1,)), ((), ())), preferred_element_type=jnp.float32
    )


def sum_chunk(copies, chunk, colour, p_ref, total, wide, kept, narrow, unit, others):
    d1, d2, d3 = COLOURS[colour]
    pos = copies.pos
    a, b = pos[d1], pos[d2]
    base = 48 * chunk + 16 * colour
    c = 3 * chunk + colour
    steps = (2, 1, 3)

    def row(i):
        return pl.ds(base + 4 * i, 4)

    sent = [
        copies.send(p_ref.at[row((a + step) % 4)], wide.at[c, slot], d1, step)
        for slot, step in enumerate(steps)
    ]
    yield
    for copy in sent:
        copy.wait_recv()
    kept[c] = (p_ref[row(a)] + wide[c, 0]) + (wide[c, 1] + wide[c, 2])
    sent = [
        copies.send(kept.at[c, (b + step) % 4], narrow.at[c, slot], d2, step)
        for slot, step in enumerate(steps)
    ]
    yield
    for copy in sent:
        copy.wait_recv()
    unit[c] = (kept[c, b] + narrow[c, 0]) + (narrow[c, 1] + narrow[c, 2])
    sent = [
        copies.send(unit.at[c], others.at[c, slot], d3, step) for slot, step in enumerate(steps)
    ]
    yield
    for copy in sent:
        copy.wait_recv()
    mine = base + 4 * a + b
    total[mine] = (unit[c] + others[c, 0]) + (others[c, 1] + others[c, 2])
    sent = [copies.send(total.at[mine], total.at[mine], d2, step) for step in steps]
    yield
    for copy in sent:
        copy.wait_recv()

    def block(q, h):
        return total.at[pl.ds(base + 4 * q + 2 * h, 2)]

    yield from gather_ring(copies, d1, lambda h: block(a, h), block)


def kernel(
    scale, count_all, x_hbm, labels_ref, proj_hbm, phase_ref, w_hbm, v_hbm, w_ref, v_ref,
    x_ref, everyone, proj_ref, p_high, p_low, f_high, f_low, a_stack, p_ref, p_next, total,
    wide, kept, narrow, unit, others, r_stack, g_ref, g_other, squares, square_parts,
    send_sems, recv_sems, pair_send, pair_recv, load_sems,
):
    pos = positions()
    classes, width = w_ref.shape
    depth = x_hbm.shape[1]
    frames = f_high.shape[0]
    partner = {"frame": 1 - lax.axis_index("frame")}
    load_x = pltpu.make_async_copy(x_hbm, x_ref, load_sems.at[0])
    load_proj = pltpu.make_async_copy(proj_hbm, proj_ref, load_sems.at[1])
    load_w = pltpu.make_async_copy(w_hbm, w_ref, load_sems.at[2])
    load_v = pltpu.make_async_copy(v_hbm, v_ref, load_sems.at[3])
    for load in (load_x, load_proj, load_w, load_v):
        load.start()

    copies = Copies(pos, send_sems, recv_sems, 0)
    barrier = pltpu.get_barrier_semaphore()
    peers = [partner] + [copies.device(dim, step) for dim in "zxy" for step in (1, 2, 3)]
    for peer in peers:
        pl.semaphore_signal(barrier, inc=1, device_id=peer, device_id_type=MESH)
    load_x.wait()
    lane = lax.broadcasted_iota(jnp.int32, (x_ref.shape[0], everyone.shape[4]), 1)
    here = (pos["z"], pos["x"], pos["y"])
    everyone[here] = jnp.where((lane == depth) | (lane == depth + 1), 1.0, 0.0)
    everyone[here + (slice(None), pl.ds(0, depth))] = x_ref[...]
    pl.semaphore_wait(barrier, len(peers))

    def piece(dims, colour, done, q, h):
        at = tuple(
            slice(None) if name in done else (q if name == dims[len(done)] else pos[name])
            for name in "zxy"
        )
        return everyone.at[at + (pl.ds(16 * colour + 8 * h, 8),)]

    def near(colour):
        dims = COLOURS[colour]
        mine = everyone.at[here + (pl.ds(16 * colour, 16),)]
        sent = [copies.send(mine, mine, dims[0], step) for step in (2, 1, 3)]
        yield
        for copy in sent:
            copy.wait_recv()
        block = functools.partial(piece, dims, colour, dims[:1])
        yield from gather_ring(copies, dims[1], functools.partial(block, pos[dims[1]]), block)

    def prepare_proj():
        load_proj.wait()
        whole = depth // 16 * 16
        step = 48
        for k in range(whole // step):
            at = pl.ds(k * step, step)
            p_high[at, :], p_low[at, :] = split(proj_ref[at, :] * TURN)
        phase = phase_ref[...] * TURN
        top = phase.astype(jnp.bfloat16).astype(jnp.float32)
        row = lax.broadcasted_iota(jnp.int32, (8, width), 0)
        tail = jnp.where(row == 0, top, jnp.where(row == 1, phase - top, 0.0))
        last = jnp.concatenate([proj_ref[whole:depth, :] * TURN, tail], axis=0)
        p_high[whole : whole + 16, :], p_low[whole : whole + 16, :] = split(last)
        rest = p_high.shape[0] - whole - 16
        p_high[whole + 16 :, :] = jnp.zeros((rest, width), jnp.bfloat16)
        p_low[whole + 16 :, :] = jnp.zeros((rest, width), jnp.bfloat16)

    def prepare_rest():
        a_stack[...] = jnp.zeros_like(a_stack)
        load_w.wait()
        load_v.wait()

    streams = advance_all([near(colour) for colour in range(3)])
    prepare_proj()
    streams = advance_all(streams)
    prepare_rest()
    while streams:
        streams = advance_all(streams)

    far = []
    for colour, dims in enumerate(COLOURS):
        block = functools.partial(piece, dims, colour, dims[:2])
        far.append(ring_copies(copies, dims[2], functools.partial(block, pos[dims[2]]), block))
    for slot in range(4):
        for ring in far:
            ring[slot].start()

    def features(i, carry):
        def when_arrived(step, slots):
            @pl.when(i == step)
            def _():
                for slot in slots:
                    for ring in far:
                        ring[slot].wait_recv()
                        if slot < 2:
                            ring[slot + 4].start()

        when_arrived(1, (0, 1))
        for slot in range(2, 6):
            when_arrived(slot + 2, (slot,))
        h = jnp.where((i == 1) | (i == 3) | (i == 4) | (i == 7), 1, 0)
        off = jnp.where(i < 2, 0, jnp.where(i > 5, 2, jnp.where((i == 2) | (i == 4), 3, 1)))
        rows, parts = [], []
        for colour, dims in enumerate(COLOURS):
            q = (pos[dims[2]] + off) % 4
            at = tuple(q if name == dims[2] else slice(None) for name in "zxy")
            lines = pl.ds(pl.multiple_of(16 * colour + 8 * h, 8), 8)
            parts.append(everyone[at + (lines, slice(None))].reshape(128, everyone.shape[4]))
            rows.append(pl.ds(pl.multiple_of(128 * (8 * colour + 4 * h + q), 128), 128))
        count = 128 * len(parts)
        high, low = split(jnp.concatenate(parts, axis=0))
        both = jnp.concatenate([high, low], axis=0)
        step = 256
        for n in range(width // step):
            at = pl.ds(n * step, step)
            turns = mul(both, p_high[:, at])
            turns = turns[:count] + turns[count:] + mul(high, p_low[:, at])
            turns = turns - ((turns + ROUNDER) - ROUNDER)
            quarter = 0.25 - jnp.abs(turns)
            square = quarter * quarter
            value = SINE[4]
            for coefficient in SINE[3::-1]:
                value = value * square + coefficient
            top, bottom = split(value * quarter)
            for colour in range(3):
                f_high[rows[colour], at] = top[128 * colour : 128 * (colour + 1)]
                f_low[rows[colour], at] = bottom[128 * colour : 128 * (colour + 1)]
        return carry

    lax.fori_loop(0, 8, features, 0)
    copies.wait_sends()

    def exchange(iteration, n):
        return pltpu.make_async_remote_copy(
            src_ref=g_ref.at[n],
            dst_ref=g_other.at[iteration, n],
            send_sem=pair_send.at[n],
            recv_sem=pair_recv.at[iteration, n],
            device_id=partner,
            device_id_type=MESH,
        )

    def look_ahead(momentum, n, carry):
        at = pl.ds(pl.multiple_of(n * TILE, TILE), TILE)
        high, low = split((w_ref[:, at] + momentum * v_ref[:, at]) * scale)
        a_stack[:classes, at] = high
        a_stack[CLASS_PAD : CLASS_PAD + classes, at] = low
        return carry

    def score(out_ref, n, carry):
        at = pl.ds(pl.multiple_of(n * TILE, TILE), TILE)
        both = mul_flipped(a_stack[...], f_high[at, :])
        low = mul_flipped(a_stack[:CLASS_PAD, :], f_low[at, :])
        scores = both[:CLASS_PAD] + both[CLASS_PAD:] + low
        for k in range(TILE // 128):
            part = scores[:, 128 * k : 128 * (k + 1)].reshape(4, UNIT, 128)
            out_ref[pl.ds(4 * (n * (TILE // 128) + k), 4)] = part
        return carry

    def residuals(block, carry):
        row = lax.broadcasted_iota(jnp.int32, (CLASS_PAD, 128), 0)
        scores = total[pl.ds(4 * block, 4)].reshape(CLASS_PAD, 128)
        scores = jnp.where(row < classes, scores, -jnp.inf)
        exponent = jnp.exp(scores - jnp.max(scores, axis=0, keepdims=True))
        probability = exponent / jnp.sum(exponent, axis=0, keepdims=True)
        label = labels_ref[pl.ds(block, 1), :]
        residual = (probability - jnp.where(row == label, 1.0, 0.0)) * scale
        at = pl.ds(pl.multiple_of(block * 128, 128), 128)
        r_stack[:CLASS_PAD, at], r_stack[CLASS_PAD:, at] = split(residual)
        return carry

    def gradient(iteration, chunk, n, carry):
        at = pl.ds(pl.multiple_of(n * TILE, TILE), TILE)
        rows = pl.ds(chunk * (frames // CHUNKS), frames // CHUNKS)
        both = mul(r_stack[:, rows], f_high[rows, at])
        value = both[:CLASS_PAD] + both[CLASS_PAD:]
        value = value + mul(r_stack[:CLASS_PAD, rows], f_low[rows, at])
        if chunk == 0:
            g_ref[n] = value
        else:
            g_ref[n] = g_ref[n] + value
        if chunk == CHUNKS - 1:
            exchange(iteration, n).start()
        return carry

    def streams(chunk):
        return [
            sum_chunk(copies, chunk, colour, p_ref, total, wide, kept, narrow, unit, others)
            for colour in range(3)
        ]

    def finish_step(iteration, early, late, pending):
        while early:
            early = advance_all(early)
            if early:
                late = advance_all(late)
            if pending:
                pending.pop(0)()
        blocks = frames // 128 // CHUNKS
        for work in pending:
            work()
        lax.fori_loop(0, blocks, residuals, 0)
        late = advance_all(late)
        lax.fori_loop(0, tiles, functools.partial(gradient, iteration, 0), 0)
        while late:
            late = advance_all(late)
        lax.fori_loop(blocks, 2 * blocks, residuals, 0)
        lax.fori_loop(0, tiles, functools.partial(gradient, iteration, 1), 0)

    def sum_squares(iteration, stacked):
        summed = jnp.zeros((8, TILE), jnp.float32)
        for n in range(tiles):
            exchange(iteration, n).wait_recv()
            value = g_ref[n] + g_other[iteration, n]
            if stacked:
                at = pl.ds(n * TILE, TILE)
                a_stack[:CLASS_PAD, at], a_stack[CLASS_PAD:, at] = split(value * scale)
            value = value * value
            summed = summed + jnp.sum(value.reshape(CLASS_PAD // 8, 8, TILE), axis=0)
        squares[0] = jnp.sum(
            jnp.stack([summed[:, 128 * k : 128 * (k + 1)] for k in range(TILE // 128)]), axis=0
        )

    def sum_over_chips():
        for stage, dim in enumerate("zxy"):
            sent = [
                copies.send(squares.at[stage], square_parts.at[stage, slot], dim, step)
                for slot, step in enumerate((2, 1, 3))
            ]
            yield
            for copy in sent:
                copy.wait_recv()
            squares[stage + 1] = (squares[stage] + square_parts[stage, 0]) + (
                square_parts[stage, 1] + square_parts[stage, 2]
            )

    def rate():
        square_sum = jnp.sum(squares[3], axis=(0, 1), keepdims=True)
        return STEP_RATE / jnp.sqrt(square_sum / count_all + EPSILON)

    def update(iteration, step_rate, n, carry):
        at = pl.ds(pl.multiple_of(n * TILE, TILE), TILE)
        value = g_ref[n, :classes] + g_other[iteration, n, :classes]
        speed = MOMENTUM * v_ref[:, at] - step_rate * value
        v_ref[:, at] = speed
        w_ref[:, at] = w_ref[:, at] + speed
        return carry

    def loop(first, last, body):
        lax.fori_loop(first, last, body, 0)

    tiles = width // TILE
    score_tiles = frames // TILE
    half = score_tiles // CHUNKS

    copies = Copies(pos, send_sems, recv_sems, FRAME_COPIES)
    loop(0, tiles, functools.partial(look_ahead, MOMENTUM))
    loop(0, half, functools.partial(score, p_ref))
    early = advance_all(streams(0))
    loop(half, score_tiles, functools.partial(score, p_ref))
    late = advance_all(streams(1))
    loop(0, tiles, functools.partial(look_ahead, MOMENTUM * (1.0 + MOMENTUM)))
    pending = [
        functools.partial(loop, n, n + 1, functools.partial(score, p_next))
        for n in range(score_tiles)
    ]
    finish_step(0, early, late, pending)

    copies.wait_sends()
    sum_squares(0, True)
    travel = sum_over_chips()
    for n in range(score_tiles):
        if n % 2 == 0:
            next(travel)
        loop(n, n + 1, functools.partial(score, p_ref))
    advance_all([travel])
    step_rate = rate()
    copies.wait_sends()
    for n in range(tiles):
        exchange(0, n).wait_send()
    copies = Copies(pos, send_sems, recv_sems, FRAME_COPIES)

    def combine(u, carry):
        p_ref[u] = p_next[u] - ((1.0 + MOMENTUM) * step_rate) * p_ref[u]
        return carry

    units = p_ref.shape[0]
    loop(0, units // CHUNKS, combine)
    early = advance_all(streams(0))
    loop(units // CHUNKS, units, combine)
    late = advance_all(streams(1))
    pending = [functools.partial(loop, 0, tiles, functools.partial(update, 0, step_rate))]
    finish_step(1, early, late, pending)
    sum_squares(1, False)
    for _ in sum_over_chips():
        pass
    loop(0, tiles, functools.partial(update, 1, rate()))
    copies.wait_sends()
    for n in range(tiles):
        exchange(1, n).wait_send()


def regroup(labels):
    parts = labels.reshape(4, 4, 4, 3, 2, 8)
    orders = ((3, 0, 1, 2, 4), (3, 2, 0, 1, 4), (3, 1, 0, 2, 4))
    return jnp.concatenate(
        [parts[:, :, :, c].transpose(order).reshape(8, 128) for c, order in enumerate(orders)]
    )


def on_device(frames, labels, proj, phase, class_weights, velocity):
    depth, width = proj.shape
    classes = class_weights.shape[1]
    feat_count = 64 * width
    scale = math.sqrt(2.0 / feat_count)
    count = labels.shape[0]
    f32, bf16 = jnp.float32, jnp.bfloat16
    units = count // 128 * 4
    colours = 3 * CHUNKS
    anywhere = pl.BlockSpec(memory_space=pl.ANY)
    vmem = pl.BlockSpec(memory_space=pltpu.VMEM)
    shape = jax.ShapeDtypeStruct((classes, width), f32)
    weights, speed = pl.pallas_call(
        functools.partial(kernel, scale, feat_count * classes),
        out_shape=[shape, shape],
        in_specs=[anywhere, vmem, anywhere, vmem, anywhere, anywhere],
        out_specs=[vmem, vmem],
        scratch_shapes=[
            pltpu.VMEM(frames.shape, f32),
            pltpu.VMEM((4, 4, 4, frames.shape[0], 512), f32),
            pltpu.VMEM((depth, width), f32),
            pltpu.VMEM((512, width), bf16),
            pltpu.VMEM((512, width), bf16),
            pltpu.VMEM((count, width), bf16),
            pltpu.VMEM((count, width), bf16),
            pltpu.VMEM((2 * CLASS_PAD, width), bf16),
            pltpu.VMEM((units, UNIT, 128), f32),
            pltpu.VMEM((units, UNIT, 128), f32),
            pltpu.VMEM((units, UNIT, 128), f32),
            pltpu.VMEM((colours, 3, 4, UNIT, 128), f32),
            pltpu.VMEM((colours, 4, UNIT, 128), f32),
            pltpu.VMEM((colours, 3, UNIT, 128), f32),
            pltpu.VMEM((colours, UNIT, 128), f32),
            pltpu.VMEM((colours, 3, UNIT, 128), f32),
            pltpu.VMEM((2 * CLASS_PAD, count), bf16),
            pltpu.VMEM((width // TILE, CLASS_PAD, TILE), f32),
            pltpu.VMEM((ITERS, width // TILE, CLASS_PAD, TILE), f32),
            pltpu.VMEM((4, 8, 128), f32),
            pltpu.VMEM((3, 3, 8, 128), f32),
            pltpu.SemaphoreType.DMA((FRAME_COPIES + SCORE_COPIES + SQUARE_COPIES,)),
            pltpu.SemaphoreType.DMA((FRAME_COPIES + SCORE_COPIES + SQUARE_COPIES,)),
            pltpu.SemaphoreType.DMA((width // TILE,)),
            pltpu.SemaphoreType.DMA((ITERS, width // TILE)),
            pltpu.SemaphoreType.DMA((4,)),
        ],
        compiler_params=pltpu.CompilerParams(
            collective_id=0, has_side_effects=True, vmem_limit_bytes=VMEM_LIMIT
        ),
        name="optimize",
    )(frames, regroup(labels), proj, phase.reshape(1, width), class_weights.T, velocity.T)
    return weights.T, speed.T


def solution(mesh):
    return jax.shard_map(
        on_device,
        mesh=mesh,
        in_specs=(
            P(("frame", "feat"), None),
            P("frame"),
            P(None, "feat"),
            P("feat"),
            P("feat", None),
            P("feat", None),
        ),
        out_specs=(P("feat", None), P("feat", None)),
        check_vma=False,
    )
```

```python
import functools
import math

import jax
import jax.numpy as jnp
from jax import lax
from jax.experimental import pallas as pl
from jax.experimental.pallas import tpu as pltpu
from jax.sharding import PartitionSpec as P

MOMENTUM = 0.9
STEP_RATE = 0.05
EPSILON = 1e-06
ITERS = 2
TURN = 1.0 / (2.0 * math.pi)
ROUNDER = 1.5 * 2.0**23
SINE = (
    6.283185160089458,
    -41.34165503141172,
    81.60100407300267,
    -76.54978228814288,
    39.53670602749812,
)
MESH = pl.DeviceIdType.MESH
VMEM_LIMIT = 67043328
CLASS_PAD = 160
UNIT = 40
COLOURS = (("y", "x", "z"), ("x", "z", "y"), ("z", "y", "x"))
FRAME_COPIES = 3 * (3 + 6 + 6)
CHUNKS = 2
SCORE_COPIES = CHUNKS * 3 * (3 + 3 + 3 + 3 + 6)
SQUARE_COPIES = 9
TILE = 512


def positions():
    index = lax.axis_index("feat")
    return {"z": index // 16, "x": (index // 4) % 4, "y": index % 4}


class Copies:
    def __init__(self, pos, send_sems, recv_sems, first):
        self.pos, self.send_sems, self.recv_sems = pos, send_sems, recv_sems
        self.slot, self.made = first, []

    def device(self, dim, step):
        moved = dict(self.pos)
        moved[dim] = (self.pos[dim] + step) % 4
        return {"feat": moved["z"] * 16 + moved["x"] * 4 + moved["y"]}

    def make(self, src, dst, dim, step):
        slot = self.slot
        self.slot += 1
        copy = pltpu.make_async_remote_copy(
            src_ref=src,
            dst_ref=dst,
            send_sem=self.send_sems.at[slot],
            recv_sem=self.recv_sems.at[slot],
            device_id=self.device(dim, step),
            device_id_type=MESH,
        )
        self.made.append(copy)
        return copy

    def send(self, src, dst, dim, step):
        copy = self.make(src, dst, dim, step)
        copy.start()
        return copy

    def wait_sends(self):
        for copy in self.made:
            copy.wait_send()
        self.made = []


def ring_copies(copies, dim, source, block):
    here = copies.pos[dim]
    before, after = (here + 3) % 4, (here + 1) % 4
    return (
        copies.make(source(0), block(here, 0), dim, 1),
        copies.make(source(1), block(here, 1), dim, 3),
        copies.make(source(1), block(here, 1), dim, 1),
        copies.make(source(0), block(here, 0), dim, 3),
        copies.make(block(before, 0), block(before, 0), dim, 1),
        copies.make(block(after, 1), block(after, 1), dim, 3),
    )


def gather_ring(copies, dim, source, block):
    ring = ring_copies(copies, dim, source, block)
    for copy in ring[:4]:
        copy.start()
    yield
    ring[0].wait_recv()
    ring[4].start()
    ring[1].wait_recv()
    ring[5].start()
    yield
    for copy in ring[2:]:
        copy.wait_recv()


def advance_all(streams):
    alive = []
    for stream in streams:
        try:
            next(stream)
            alive.append(stream)
        except StopIteration:
            pass
    return alive


def split(value):
    high = value.astype(jnp.bfloat16)
    return high, (value - high.astype(jnp.float32)).astype(jnp.bfloat16)


def mul(left, right):
    return jnp.dot(left, right, preferred_element_type=jnp.float32)


def mul_flipped(left, right):
    return lax.dot_general(
        left, right, (((1,), (1,)), ((), ())), preferred_element_type=jnp.float32
    )


def sum_chunk(copies, chunk, colour, p_ref, total, wide, kept, narrow, unit, others):
    d1, d2, d3 = COLOURS[colour]
    pos = copies.pos
    a, b = pos[d1], pos[d2]
    base = 48 * chunk + 16 * colour
    c = 3 * chunk + colour
    steps = (2, 1, 3)

    def row(i):
        return pl.ds(base + 4 * i, 4)

    sent = [
        copies.send(p_ref.at[row((a + step) % 4)], wide.at[c, slot], d1, step)
        for slot, step in enumerate(steps)
    ]
    yield
    for copy in sent:
        copy.wait_recv()
    kept[c] = (p_ref[row(a)] + wide[c, 0]) + (wide[c, 1] + wide[c, 2])
    sent = [
        copies.send(kept.at[c, (b + step) % 4], narrow.at[c, slot], d2, step)
        for slot, step in enumerate(steps)
    ]
    yield
    for copy in sent:
        copy.wait_recv()
    unit[c] = (kept[c, b] + narrow[c, 0]) + (narrow[c, 1] + narrow[c, 2])
    sent = [
        copies.send(unit.at[c], others.at[c, slot], d3, step) for slot, step in enumerate(steps)
    ]
    yield
    for copy in sent:
        copy.wait_recv()
    mine = base + 4 * a + b
    total[mine] = (unit[c] + others[c, 0]) + (others[c, 1] + others[c, 2])
    sent = [copies.send(total.at[mine], total.at[mine], d2, step) for step in steps]
    yield
    for copy in sent:
        copy.wait_recv()

    def block(q, h):
        return total.at[pl.ds(base + 4 * q + 2 * h, 2)]

    yield from gather_ring(copies, d1, lambda h: block(a, h), block)


def kernel(
    scale, count_all, x_hbm, labels_ref, proj_hbm, phase_ref, w_hbm, v_hbm, w_ref, v_ref,
    label_rows, x_ref, everyone, proj_ref, p_high, p_low, f_high, f_low, a_stack, p_ref, p_next, total,
    wide, kept, narrow, unit, others, r_stack, g_ref, g_other, squares, square_parts,
    send_sems, recv_sems, pair_send, pair_recv, load_sems,
):
    pos = positions()
    classes, width = w_ref.shape
    depth = x_hbm.shape[1]
    frames = f_high.shape[0]
    partner = {"frame": 1 - lax.axis_index("frame")}
    load_x = pltpu.make_async_copy(x_hbm, x_ref, load_sems.at[0])
    load_proj = pltpu.make_async_copy(proj_hbm, proj_ref, load_sems.at[1])
    load_w = pltpu.make_async_copy(w_hbm, w_ref, load_sems.at[2])
    load_v = pltpu.make_async_copy(v_hbm, v_ref, load_sems.at[3])
    for load in (load_x, load_proj, load_w, load_v):
        load.start()

    copies = Copies(pos, send_sems, recv_sems, 0)
    barrier = pltpu.get_barrier_semaphore()
    peers = [partner] + [copies.device(dim, step) for dim in "zxy" for step in (1, 2, 3)]
    for peer in peers:
        pl.semaphore_signal(barrier, inc=1, device_id=peer, device_id_type=MESH)
    load_x.wait()
    lane = lax.broadcasted_iota(jnp.int32, (x_ref.shape[0], everyone.shape[4]), 1)
    here = (pos["z"], pos["x"], pos["y"])
    everyone[here] = jnp.where((lane == depth) | (lane == depth + 1), 1.0, 0.0)
    everyone[here + (slice(None), pl.ds(0, depth))] = x_ref[...]
    pl.semaphore_wait(barrier, len(peers))

    def piece(dims, colour, done, q, h):
        at = tuple(
            slice(None) if name in done else (q if name == dims[len(done)] else pos[name])
            for name in "zxy"
        )
        return everyone.at[at + (pl.ds(16 * colour + 8 * h, 8),)]

    def near(colour):
        dims = COLOURS[colour]
        mine = everyone.at[here + (pl.ds(16 * colour, 16),)]
        sent = [copies.send(mine, mine, dims[0], step) for step in (2, 1, 3)]
        yield
        for copy in sent:
            copy.wait_recv()
        block = functools.partial(piece, dims, colour, dims[:1])
        yield from gather_ring(copies, dims[1], functools.partial(block, pos[dims[1]]), block)

    def prepare_proj():
        load_proj.wait()
        whole = depth // 16 * 16
        step = 48
        for k in range(whole // step):
            at = pl.ds(k * step, step)
            p_high[at, :], p_low[at, :] = split(proj_ref[at, :] * TURN)
        phase = phase_ref[...] * TURN
        top = phase.astype(jnp.bfloat16).astype(jnp.float32)
        row = lax.broadcasted_iota(jnp.int32, (8, width), 0)
        tail = jnp.where(row == 0, top, jnp.where(row == 1, phase - top, 0.0))
        last = jnp.concatenate([proj_ref[whole:depth, :] * TURN, tail], axis=0)
        p_high[whole : whole + 16, :], p_low[whole : whole + 16, :] = split(last)
        rest = p_high.shape[0] - whole - 16
        p_high[whole + 16 :, :] = jnp.zeros((rest, width), jnp.bfloat16)
        p_low[whole + 16 :, :] = jnp.zeros((rest, width), jnp.bfloat16)

    def prepare_rest():
        a_stack[...] = jnp.zeros_like(a_stack)
        load_w.wait()
        load_v.wait()

    streams = advance_all([near(colour) for colour in range(3)])
    prepare_proj()
    streams = advance_all(streams)
    prepare_rest()
    while streams:
        streams = advance_all(streams)

    far = []
    for colour, dims in enumerate(COLOURS):
        block = functools.partial(piece, dims, colour, dims[:2])
        far.append(ring_copies(copies, dims[2], functools.partial(block, pos[dims[2]]), block))
    for slot in range(4):
        for ring in far:
            ring[slot].start()

    def features(i, carry):
        def when_arrived(step, slots):
            @pl.when(i == step)
            def _():
                for slot in slots:
                    for ring in far:
                        ring[slot].wait_recv()
                        if slot < 2:
                            ring[slot + 4].start()

        when_arrived(1, (0, 1))
        for slot in range(2, 6):
            when_arrived(slot + 2, (slot,))
        h = jnp.where((i == 1) | (i == 3) | (i == 4) | (i == 7), 1, 0)
        off = jnp.where(i < 2, 0, jnp.where(i > 5, 2, jnp.where((i == 2) | (i == 4), 3, 1)))
        rows, parts = [], []
        for colour, dims in enumerate(COLOURS):
            q = (pos[dims[2]] + off) % 4
            at = tuple(q if name == dims[2] else slice(None) for name in "zxy")
            lines = pl.ds(pl.multiple_of(16 * colour + 8 * h, 8), 8)
            parts.append(everyone[at + (lines, slice(None))].reshape(128, everyone.shape[4]))
            rows.append(pl.ds(pl.multiple_of(128 * (8 * colour + 4 * h + q), 128), 128))
        count = 128 * len(parts)
        high, low = split(jnp.concatenate(parts, axis=0))
        both = jnp.concatenate([high, low], axis=0)
        step = 256
        for n in range(width // step):
            at = pl.ds(n * step, step)
            turns = mul(both, p_high[:, at])
            turns = turns[:count] + turns[count:] + mul(high, p_low[:, at])
            turns = turns - ((turns + ROUNDER) - ROUNDER)
            quarter = 0.25 - jnp.abs(turns)
            square = quarter * quarter
            value = SINE[4]
            for coefficient in SINE[3::-1]:
                value = value * square + coefficient
            top, bottom = split(value * quarter)
            for colour in range(3):
                f_high[rows[colour], at] = top[128 * colour : 128 * (colour + 1)]
                f_low[rows[colour], at] = bottom[128 * colour : 128 * (colour + 1)]
        return carry

    lax.fori_loop(0, 8, features, 0)
    copies.wait_sends()

    def exchange(iteration, n):
        return pltpu.make_async_remote_copy(
            src_ref=g_ref.at[n],
            dst_ref=g_other.at[iteration, n],
            send_sem=pair_send.at[n],
            recv_sem=pair_recv.at[iteration, n],
            device_id=partner,
            device_id_type=MESH,
        )

    def look_ahead(momentum, n, carry):
        at = pl.ds(pl.multiple_of(n * TILE, TILE), TILE)
        high, low = split((w_ref[:, at] + momentum * v_ref[:, at]) * scale)
        a_stack[:classes, at] = high
        a_stack[CLASS_PAD : CLASS_PAD + classes, at] = low
        return carry

    def score(out_ref, n, carry):
        at = pl.ds(pl.multiple_of(n * TILE, TILE), TILE)
        both = mul_flipped(a_stack[...], f_high[at, :])
        low = mul_flipped(a_stack[:CLASS_PAD, :], f_low[at, :])
        scores = both[:CLASS_PAD] + both[CLASS_PAD:] + low
        for k in range(TILE // 128):
            part = scores[:, 128 * k : 128 * (k + 1)].reshape(4, UNIT, 128)
            out_ref[pl.ds(4 * (n * (TILE // 128) + k), 4)] = part
        return carry

    def residuals(block, carry):
        row = lax.broadcasted_iota(jnp.int32, (CLASS_PAD, 128), 0)
        number = row.astype(jnp.float32)
        scores = total[pl.ds(4 * block, 4)].reshape(CLASS_PAD, 128)
        scores = jnp.where(row < classes, scores, -jnp.inf)
        exponent = jnp.exp(scores - jnp.max(scores, axis=0, keepdims=True))
        probability = exponent / jnp.sum(exponent, axis=0, keepdims=True)
        label = label_rows[pl.ds(block, 1), :]
        residual = (probability - jnp.where(number == label, 1.0, 0.0)) * scale
        at = pl.ds(pl.multiple_of(block * 128, 128), 128)
        r_stack[:CLASS_PAD, at], r_stack[CLASS_PAD:, at] = split(residual)
        return carry

    def gradient(iteration, chunk, n, carry):
        at = pl.ds(pl.multiple_of(n * TILE, TILE), TILE)
        rows = pl.ds(chunk * (frames // CHUNKS), frames // CHUNKS)
        both = mul(r_stack[:, rows], f_high[rows, at])
        value = both[:CLASS_PAD] + both[CLASS_PAD:]
        value = value + mul(r_stack[:CLASS_PAD, rows], f_low[rows, at])
        if chunk == 0:
            g_ref[n] = value
        else:
            g_ref[n] = g_ref[n] + value
        if chunk == CHUNKS - 1:
            exchange(iteration, n).start()
        return carry

    def streams(chunk):
        return [
            sum_chunk(copies, chunk, colour, p_ref, total, wide, kept, narrow, unit, others)
            for colour in range(3)
        ]

    def finish_step(iteration, early, late, pending):
        while early:
            early = advance_all(early)
            if early:
                late = advance_all(late)
            if pending:
                pending.pop(0)()
        blocks = frames // 128 // CHUNKS
        for work in pending:
            work()
        lax.fori_loop(0, blocks, residuals, 0)
        late = advance_all(late)
        lax.fori_loop(0, tiles, functools.partial(gradient, iteration, 0), 0)
        while late:
            late = advance_all(late)
        lax.fori_loop(blocks, 2 * blocks, residuals, 0)
        lax.fori_loop(0, tiles, functools.partial(gradient, iteration, 1), 0)

    def sum_squares(iteration, stacked):
        summed = jnp.zeros((8, TILE), jnp.float32)
        for n in range(tiles):
            exchange(iteration, n).wait_recv()
            value = g_ref[n] + g_other[iteration, n]
            if stacked:
                at = pl.ds(n * TILE, TILE)
                a_stack[:CLASS_PAD, at], a_stack[CLASS_PAD:, at] = split(value * scale)
            value = value * value
            summed = summed + jnp.sum(value.reshape(CLASS_PAD // 8, 8, TILE), axis=0)
        squares[0] = jnp.sum(
            jnp.stack([summed[:, 128 * k : 128 * (k + 1)] for k in range(TILE // 128)]), axis=0
        )

    def sum_over_chips():
        for stage, dim in enumerate("zxy"):
            sent = [
                copies.send(squares.at[stage], square_parts.at[stage, slot], dim, step)
                for slot, step in enumerate((2, 1, 3))
            ]
            yield
            for copy in sent:
                copy.wait_recv()
            squares[stage + 1] = (squares[stage] + square_parts[stage, 0]) + (
                square_parts[stage, 1] + square_parts[stage, 2]
            )

    def rate():
        square_sum = jnp.sum(squares[3], axis=(0, 1), keepdims=True)
        return STEP_RATE / jnp.sqrt(square_sum / count_all + EPSILON)

    def update(iteration, step_rate, n, carry):
        at = pl.ds(pl.multiple_of(n * TILE, TILE), TILE)
        value = g_ref[n, :classes] + g_other[iteration, n, :classes]
        speed = MOMENTUM * v_ref[:, at] - step_rate * value
        v_ref[:, at] = speed
        w_ref[:, at] = w_ref[:, at] + speed
        return carry

    def order_labels():
        groups = frames // 8
        held = labels_ref[...].astype(jnp.float32)
        held = jnp.concatenate([held, jnp.zeros((128 - held.shape[0], 128), jnp.float32)], axis=0)
        group = lax.broadcasted_iota(jnp.int32, (groups, 128), 0)
        lane = lax.broadcasted_iota(jnp.int32, (groups, 128), 1)
        picks = jnp.where((group >> 4) == lane, 1.0, 0.0).astype(jnp.bfloat16)
        spread = mul(picks, held.astype(jnp.bfloat16))
        spread = jnp.where((lane >> 3) == (group & 15), spread, 0.0).astype(jnp.bfloat16)
        line = lax.broadcasted_iota(jnp.int32, (128, 128), 0)
        column = lax.broadcasted_iota(jnp.int32, (128, 128), 1)
        same = jnp.where((line & 7) == (column & 7), 1.0, 0.0).astype(jnp.bfloat16)
        spread = mul(spread, same)
        place = lane >> 3
        for colour in range(3):
            for h in range(2):
                for q in range(4):
                    device = (
                        16 * q + place,
                        4 * place + q,
                        16 * (place >> 2) + 4 * q + (place & 3),
                    )[colour]
                    chosen = jnp.where(group == 6 * device + 2 * colour + h, spread, 0.0)
                    block = 8 * colour + 4 * h + q
                    label_rows[block : block + 1, :] = jnp.sum(chosen, axis=0, keepdims=True)

    def loop(first, last, body):
        lax.fori_loop(first, last, body, 0)

    tiles = width // TILE
    score_tiles = frames // TILE
    half = score_tiles // CHUNKS

    copies = Copies(pos, send_sems, recv_sems, FRAME_COPIES)
    loop(0, tiles, functools.partial(look_ahead, MOMENTUM))
    loop(0, half, functools.partial(score, p_ref))
    early = advance_all(streams(0))
    loop(half, score_tiles, functools.partial(score, p_ref))
    late = advance_all(streams(1))
    loop(0, tiles, functools.partial(look_ahead, MOMENTUM * (1.0 + MOMENTUM)))
    pending = [
        functools.partial(loop, n, n + 1, functools.partial(score, p_next))
        for n in range(score_tiles)
    ]
    finish_step(0, early, late, [order_labels] + pending)

    copies.wait_sends()
    sum_squares(0, True)
    travel = sum_over_chips()
    for n in range(half):
        next(travel)
        loop(n, n + 1, functools.partial(score, p_ref))
    advance_all([travel])
    step_rate = rate()
    copies.wait_sends()
    for n in range(tiles):
        exchange(0, n).wait_send()
    copies = Copies(pos, send_sems, recv_sems, FRAME_COPIES)

    def combine(u, carry):
        p_ref[u] = p_next[u] - ((1.0 + MOMENTUM) * step_rate) * p_ref[u]
        return carry

    units = p_ref.shape[0]
    loop(0, units // CHUNKS, combine)
    early = advance_all(streams(0))
    loop(half, score_tiles, functools.partial(score, p_ref))
    loop(units // CHUNKS, units, combine)
    late = advance_all(streams(1))
    pending = [functools.partial(loop, 0, tiles, functools.partial(update, 0, step_rate))]
    finish_step(1, early, late, pending)
    sum_squares(1, False)
    for _ in sum_over_chips():
        pass
    loop(0, tiles, functools.partial(update, 1, rate()))
    copies.wait_sends()
    for n in range(tiles):
        exchange(1, n).wait_send()


def on_device(frames, labels, proj, phase, class_weights, velocity):
    depth, width = proj.shape
    classes = class_weights.shape[1]
    feat_count = 64 * width
    scale = math.sqrt(2.0 / feat_count)
    count = labels.shape[0]
    f32, bf16 = jnp.float32, jnp.bfloat16
    units = count // 128 * 4
    colours = 3 * CHUNKS
    anywhere = pl.BlockSpec(memory_space=pl.ANY)
    vmem = pl.BlockSpec(memory_space=pltpu.VMEM)
    shape = jax.ShapeDtypeStruct((classes, width), f32)
    weights, speed = pl.pallas_call(
        functools.partial(kernel, scale, feat_count * classes),
        out_shape=[shape, shape],
        in_specs=[anywhere, vmem, anywhere, vmem, anywhere, anywhere],
        out_specs=[vmem, vmem],
        scratch_shapes=[
            pltpu.VMEM((count // 128, 128), f32),
            pltpu.VMEM(frames.shape, f32),
            pltpu.VMEM((4, 4, 4, frames.shape[0], 512), f32),
            pltpu.VMEM((depth, width), f32),
            pltpu.VMEM((512, width), bf16),
            pltpu.VMEM((512, width), bf16),
            pltpu.VMEM((count, width), bf16),
            pltpu.VMEM((count, width), bf16),
            pltpu.VMEM((2 * CLASS_PAD, width), bf16),
            pltpu.VMEM((units, UNIT, 128), f32),
            pltpu.VMEM((units, UNIT, 128), f32),
            pltpu.VMEM((units, UNIT, 128), f32),
            pltpu.VMEM((colours, 3, 4, UNIT, 128), f32),
            pltpu.VMEM((colours, 4, UNIT, 128), f32),
            pltpu.VMEM((colours, 3, UNIT, 128), f32),
            pltpu.VMEM((colours, UNIT, 128), f32),
            pltpu.VMEM((colours, 3, UNIT, 128), f32),
            pltpu.VMEM((2 * CLASS_PAD, count), bf16),
            pltpu.VMEM((width // TILE, CLASS_PAD, TILE), f32),
            pltpu.VMEM((ITERS, width // TILE, CLASS_PAD, TILE), f32),
            pltpu.VMEM((4, 8, 128), f32),
            pltpu.VMEM((3, 3, 8, 128), f32),
            pltpu.SemaphoreType.DMA((FRAME_COPIES + SCORE_COPIES + SQUARE_COPIES,)),
            pltpu.SemaphoreType.DMA((FRAME_COPIES + SCORE_COPIES + SQUARE_COPIES,)),
            pltpu.SemaphoreType.DMA((width // TILE,)),
            pltpu.SemaphoreType.DMA((ITERS, width // TILE)),
            pltpu.SemaphoreType.DMA((4,)),
        ],
        compiler_params=pltpu.CompilerParams(
            collective_id=0, has_side_effects=True, vmem_limit_bytes=VMEM_LIMIT
        ),
        name="optimize",
    )(frames, labels.reshape(count // 128, 128), proj, phase.reshape(1, width), class_weights.T, velocity.T)
    return weights.T, speed.T


def solution(mesh):
    return jax.shard_map(
        on_device,
        mesh=mesh,
        in_specs=(
            P(("frame", "feat"), None),
            P("frame"),
            P(None, "feat"),
            P("feat"),
            P("feat", None),
            P("feat", None),
        ),
        out_specs=(P("feat", None), P("feat", None)),
        check_vma=False,
    )
```

```python
import functools
import math

import jax
import jax.numpy as jnp
from jax import lax
from jax.experimental import pallas as pl
from jax.experimental.pallas import tpu as pltpu
from jax.sharding import PartitionSpec as P

MOMENTUM = 0.9
STEP_RATE = 0.05
EPSILON = 1e-06
ITERS = 2
TURN = 1.0 / (2.0 * math.pi)
ROUNDER = 1.5 * 2.0**23
SINE = (
    6.283185160089458,
    -41.34165503141172,
    81.60100407300267,
    -76.54978228814288,
    39.53670602749812,
)
MESH = pl.DeviceIdType.MESH
VMEM_LIMIT = 67043328
CLASS_PAD = 160
UNIT = 40
COLOURS = (("y", "x", "z"), ("x", "z", "y"), ("z", "y", "x"))
FRAME_COPIES = 3 * (3 + 6 + 6)
CHUNKS = 2
SCORE_COPIES = CHUNKS * 3 * (3 + 3 + 3 + 3 + 6)
SQUARE_COPIES = 9
TILE = 512


def positions():
    index = lax.axis_index("feat")
    return {"z": index // 16, "x": (index // 4) % 4, "y": index % 4}


class Copies:
    def __init__(self, pos, send_sems, recv_sems, first):
        self.pos, self.send_sems, self.recv_sems = pos, send_sems, recv_sems
        self.slot, self.made = first, []

    def device(self, dim, step):
        moved = dict(self.pos)
        moved[dim] = (self.pos[dim] + step) % 4
        return {"feat": moved["z"] * 16 + moved["x"] * 4 + moved["y"]}

    def make(self, src, dst, dim, step):
        slot = self.slot
        self.slot += 1
        copy = pltpu.make_async_remote_copy(
            src_ref=src,
            dst_ref=dst,
            send_sem=self.send_sems.at[slot],
            recv_sem=self.recv_sems.at[slot],
            device_id=self.device(dim, step),
            device_id_type=MESH,
        )
        self.made.append(copy)
        return copy

    def send(self, src, dst, dim, step):
        copy = self.make(src, dst, dim, step)
        copy.start()
        return copy

    def wait_sends(self):
        for copy in self.made:
            copy.wait_send()
        self.made = []


def ring_copies(copies, dim, source, block):
    here = copies.pos[dim]
    before, after = (here + 3) % 4, (here + 1) % 4
    return (
        copies.make(source(0), block(here, 0), dim, 1),
        copies.make(source(1), block(here, 1), dim, 3),
        copies.make(source(1), block(here, 1), dim, 1),
        copies.make(source(0), block(here, 0), dim, 3),
        copies.make(block(before, 0), block(before, 0), dim, 1),
        copies.make(block(after, 1), block(after, 1), dim, 3),
    )


def gather_ring(copies, dim, source, block):
    ring = ring_copies(copies, dim, source, block)
    for copy in ring[:4]:
        copy.start()
    yield
    ring[0].wait_recv()
    ring[4].start()
    ring[1].wait_recv()
    ring[5].start()
    yield
    for copy in ring[2:]:
        copy.wait_recv()


def advance_all(streams):
    alive = []
    for stream in streams:
        try:
            next(stream)
            alive.append(stream)
        except StopIteration:
            pass
    return alive


def split(value):
    high = value.astype(jnp.bfloat16)
    return high, (value - high.astype(jnp.float32)).astype(jnp.bfloat16)


def mul(left, right):
    return jnp.dot(left, right, preferred_element_type=jnp.float32)


def mul_flipped(left, right):
    return lax.dot_general(
        left, right, (((1,), (1,)), ((), ())), preferred_element_type=jnp.float32
    )


def sum_chunk(copies, chunk, colour, p_ref, total, wide, kept, narrow, unit, others):
    d1, d2, d3 = COLOURS[colour]
    pos = copies.pos
    a, b = pos[d1], pos[d2]
    base = 48 * chunk + 16 * colour
    c = 3 * chunk + colour
    steps = (2, 1, 3)

    def row(i):
        return pl.ds(base + 4 * i, 4)

    sent = [
        copies.send(p_ref.at[row((a + step) % 4)], wide.at[c, slot], d1, step)
        for slot, step in enumerate(steps)
    ]
    yield
    for copy in sent:
        copy.wait_recv()
    kept[c] = (p_ref[row(a)] + wide[c, 0]) + (wide[c, 1] + wide[c, 2])
    sent = [
        copies.send(kept.at[c, (b + step) % 4], narrow.at[c, slot], d2, step)
        for slot, step in enumerate(steps)
    ]
    yield
    for copy in sent:
        copy.wait_recv()
    unit[c] = (kept[c, b] + narrow[c, 0]) + (narrow[c, 1] + narrow[c, 2])
    sent = [
        copies.send(unit.at[c], others.at[c, slot], d3, step) for slot, step in enumerate(steps)
    ]
    yield
    for copy in sent:
        copy.wait_recv()
    mine = base + 4 * a + b
    total[mine] = (unit[c] + others[c, 0]) + (others[c, 1] + others[c, 2])
    sent = [copies.send(total.at[mine], total.at[mine], d2, step) for step in steps]
    yield
    for copy in sent:
        copy.wait_recv()

    def block(q, h):
        return total.at[pl.ds(base + 4 * q + 2 * h, 2)]

    yield from gather_ring(copies, d1, lambda h: block(a, h), block)


def kernel(
    scale, count_all, x_hbm, labels_ref, proj_hbm, phase_ref, w_hbm, v_hbm, w_ref, v_ref,
    label_rows, x_ref, everyone, proj_ref, p_high, p_low, f_high, f_low, a_stack, p_ref, p_next, total,
    wide, kept, narrow, unit, others, r_stack, g_ref, g_other, squares, square_parts,
    send_sems, recv_sems, pair_send, pair_recv, load_sems,
):
    pos = positions()
    classes, width = w_ref.shape
    depth = x_hbm.shape[1]
    frames = f_high.shape[0]
    partner = {"frame": 1 - lax.axis_index("frame")}
    load_x = pltpu.make_async_copy(x_hbm, x_ref, load_sems.at[0])
    load_proj = pltpu.make_async_copy(proj_hbm, proj_ref, load_sems.at[1])
    load_w = pltpu.make_async_copy(w_hbm, w_ref, load_sems.at[2])
    load_v = pltpu.make_async_copy(v_hbm, v_ref, load_sems.at[3])
    for load in (load_x, load_proj, load_w, load_v):
        load.start()

    copies = Copies(pos, send_sems, recv_sems, 0)
    barrier = pltpu.get_barrier_semaphore()
    peers = [partner] + [copies.device(dim, step) for dim in "zxy" for step in (1, 2, 3)]
    for peer in peers:
        pl.semaphore_signal(barrier, inc=1, device_id=peer, device_id_type=MESH)
    load_x.wait()
    lane = lax.broadcasted_iota(jnp.int32, (x_ref.shape[0], everyone.shape[4]), 1)
    here = (pos["z"], pos["x"], pos["y"])
    everyone[here] = jnp.where((lane == depth) | (lane == depth + 1), 1.0, 0.0)
    everyone[here + (slice(None), pl.ds(0, depth))] = x_ref[...]
    pl.semaphore_wait(barrier, len(peers))

    def piece(dims, colour, done, q, h):
        at = tuple(
            slice(None) if name in done else (q if name == dims[len(done)] else pos[name])
            for name in "zxy"
        )
        return everyone.at[at + (pl.ds(16 * colour + 8 * h, 8),)]

    def near(colour):
        dims = COLOURS[colour]
        mine = everyone.at[here + (pl.ds(16 * colour, 16),)]
        sent = [copies.send(mine, mine, dims[0], step) for step in (2, 1, 3)]
        yield
        for copy in sent:
            copy.wait_recv()
        block = functools.partial(piece, dims, colour, dims[:1])
        yield from gather_ring(copies, dims[1], functools.partial(block, pos[dims[1]]), block)

    def prepare_proj():
        load_proj.wait()
        whole = depth // 16 * 16
        step = 48
        for k in range(whole // step):
            at = pl.ds(k * step, step)
            p_high[at, :], p_low[at, :] = split(proj_ref[at, :] * TURN)
        phase = phase_ref[...] * TURN
        top = phase.astype(jnp.bfloat16).astype(jnp.float32)
        row = lax.broadcasted_iota(jnp.int32, (8, width), 0)
        tail = jnp.where(row == 0, top, jnp.where(row == 1, phase - top, 0.0))
        last = jnp.concatenate([proj_ref[whole:depth, :] * TURN, tail], axis=0)
        p_high[whole : whole + 16, :], p_low[whole : whole + 16, :] = split(last)
        rest = p_high.shape[0] - whole - 16
        p_high[whole + 16 :, :] = jnp.zeros((rest, width), jnp.bfloat16)
        p_low[whole + 16 :, :] = jnp.zeros((rest, width), jnp.bfloat16)

    def prepare_rest():
        a_stack[...] = jnp.zeros_like(a_stack)
        load_w.wait()
        load_v.wait()

    def order_labels():
        groups = frames // 8
        held = labels_ref[...].astype(jnp.float32)
        held = jnp.concatenate([held, jnp.zeros((128 - held.shape[0], 128), jnp.float32)], axis=0)
        group = lax.broadcasted_iota(jnp.int32, (groups, 128), 0)
        lane = lax.broadcasted_iota(jnp.int32, (groups, 128), 1)
        picks = jnp.where((group >> 4) == lane, 1.0, 0.0).astype(jnp.bfloat16)
        spread = mul(picks, held.astype(jnp.bfloat16))
        spread = jnp.where((lane >> 3) == (group & 15), spread, 0.0).astype(jnp.bfloat16)
        line = lax.broadcasted_iota(jnp.int32, (128, 128), 0)
        column = lax.broadcasted_iota(jnp.int32, (128, 128), 1)
        same = jnp.where((line & 7) == (column & 7), 1.0, 0.0).astype(jnp.bfloat16)
        spread = mul(spread, same)
        place = lane >> 3
        for colour in range(3):
            for h in range(2):
                for q in range(4):
                    device = (
                        16 * q + place,
                        4 * place + q,
                        16 * (place >> 2) + 4 * q + (place & 3),
                    )[colour]
                    chosen = jnp.where(group == 6 * device + 2 * colour + h, spread, 0.0)
                    block = 8 * colour + 4 * h + q
                    label_rows[block : block + 1, :] = jnp.sum(chosen, axis=0, keepdims=True)

    streams = advance_all([near(colour) for colour in range(3)])
    prepare_proj()
    streams = advance_all(streams)
    prepare_rest()
    streams = advance_all(streams)
    order_labels()
    while streams:
        streams = advance_all(streams)

    far = []
    for colour, dims in enumerate(COLOURS):
        block = functools.partial(piece, dims, colour, dims[:2])
        far.append(ring_copies(copies, dims[2], functools.partial(block, pos[dims[2]]), block))
    for slot in range(4):
        for ring in far:
            ring[slot].start()

    def features(i, carry):
        def when_arrived(step, slots):
            @pl.when(i == step)
            def _():
                for slot in slots:
                    for ring in far:
                        ring[slot].wait_recv()
                        if slot < 2:
                            ring[slot + 4].start()

        when_arrived(1, (0, 1))
        for slot in range(2, 6):
            when_arrived(slot + 2, (slot,))
        h = jnp.where((i == 1) | (i == 3) | (i == 4) | (i == 7), 1, 0)
        off = jnp.where(i < 2, 0, jnp.where(i > 5, 2, jnp.where((i == 2) | (i == 4), 3, 1)))
        rows, parts = [], []
        for colour, dims in enumerate(COLOURS):
            q = (pos[dims[2]] + off) % 4
            at = tuple(q if name == dims[2] else slice(None) for name in "zxy")
            lines = pl.ds(pl.multiple_of(16 * colour + 8 * h, 8), 8)
            parts.append(everyone[at + (lines, slice(None))].reshape(128, everyone.shape[4]))
            rows.append(pl.ds(pl.multiple_of(128 * (8 * colour + 4 * h + q), 128), 128))
        count = 128 * len(parts)
        high, low = split(jnp.concatenate(parts, axis=0))
        both = jnp.concatenate([high, low], axis=0)
        step = 256
        for n in range(width // step):
            at = pl.ds(n * step, step)
            turns = mul(both, p_high[:, at])
            turns = turns[:count] + turns[count:] + mul(high, p_low[:, at])
            turns = turns - ((turns + ROUNDER) - ROUNDER)
            quarter = 0.25 - jnp.abs(turns)
            square = quarter * quarter
            value = SINE[4]
            for coefficient in SINE[3::-1]:
                value = value * square + coefficient
            top, bottom = split(value * quarter)
            for colour in range(3):
                f_high[rows[colour], at] = top[128 * colour : 128 * (colour + 1)]
                f_low[rows[colour], at] = bottom[128 * colour : 128 * (colour + 1)]
        return carry

    lax.fori_loop(0, 8, features, 0)
    copies.wait_sends()

    def exchange(iteration, n):
        return pltpu.make_async_remote_copy(
            src_ref=g_ref.at[n],
            dst_ref=g_other.at[iteration, n],
            send_sem=pair_send.at[n],
            recv_sem=pair_recv.at[iteration, n],
            device_id=partner,
            device_id_type=MESH,
        )

    def look_ahead(momentum, n, carry):
        at = pl.ds(pl.multiple_of(n * TILE, TILE), TILE)
        high, low = split((w_ref[:, at] + momentum * v_ref[:, at]) * scale)
        a_stack[:classes, at] = high
        a_stack[CLASS_PAD : CLASS_PAD + classes, at] = low
        return carry

    def score(out_ref, n, carry):
        at = pl.ds(pl.multiple_of(n * TILE, TILE), TILE)
        both = mul_flipped(a_stack[...], f_high[at, :])
        low = mul_flipped(a_stack[:CLASS_PAD, :], f_low[at, :])
        scores = both[:CLASS_PAD] + both[CLASS_PAD:] + low
        for k in range(TILE // 128):
            part = scores[:, 128 * k : 128 * (k + 1)].reshape(4, UNIT, 128)
            out_ref[pl.ds(4 * (n * (TILE // 128) + k), 4)] = part
        return carry

    def residuals(block, carry):
        row = lax.broadcasted_iota(jnp.int32, (CLASS_PAD, 128), 0)
        number = row.astype(jnp.float32)
        scores = total[pl.ds(4 * block, 4)].reshape(CLASS_PAD, 128)
        scores = jnp.where(row < classes, scores, -jnp.inf)
        exponent = jnp.exp(scores - jnp.max(scores, axis=0, keepdims=True))
        probability = exponent / jnp.sum(exponent, axis=0, keepdims=True)
        label = label_rows[pl.ds(block, 1), :]
        residual = (probability - jnp.where(number == label, 1.0, 0.0)) * scale
        at = pl.ds(pl.multiple_of(block * 128, 128), 128)
        r_stack[:CLASS_PAD, at], r_stack[CLASS_PAD:, at] = split(residual)
        return carry

    def gradient(iteration, chunk, n, carry):
        at = pl.ds(pl.multiple_of(n * TILE, TILE), TILE)
        rows = pl.ds(chunk * (frames // CHUNKS), frames // CHUNKS)
        both = mul(r_stack[:, rows], f_high[rows, at])
        value = both[:CLASS_PAD] + both[CLASS_PAD:]
        value = value + mul(r_stack[:CLASS_PAD, rows], f_low[rows, at])
        if chunk == 0:
            g_ref[n] = value
        else:
            g_ref[n] = g_ref[n] + value
        if chunk == CHUNKS - 1:
            exchange(iteration, n).start()
        return carry

    def streams(chunk):
        return [
            sum_chunk(copies, chunk, colour, p_ref, total, wide, kept, narrow, unit, others)
            for colour in range(3)
        ]

    def finish_step(iteration, early, late, pending):
        while early:
            early = advance_all(early)
            if early:
                late = advance_all(late)
            if pending:
                pending.pop(0)()
        blocks = frames // 128 // CHUNKS
        for work in pending:
            work()
        lax.fori_loop(0, blocks, residuals, 0)
        late = advance_all(late)
        lax.fori_loop(0, tiles, functools.partial(gradient, iteration, 0), 0)
        while late:
            late = advance_all(late)
        lax.fori_loop(blocks, 2 * blocks, residuals, 0)
        lax.fori_loop(0, tiles, functools.partial(gradient, iteration, 1), 0)

    def sum_squares(iteration, stacked):
        summed = jnp.zeros((8, TILE), jnp.float32)
        for n in range(tiles):
            exchange(iteration, n).wait_recv()
            value = g_ref[n] + g_other[iteration, n]
            if stacked:
                at = pl.ds(n * TILE, TILE)
                a_stack[:CLASS_PAD, at], a_stack[CLASS_PAD:, at] = split(value * scale)
            value = value * value
            summed = summed + jnp.sum(value.reshape(CLASS_PAD // 8, 8, TILE), axis=0)
        squares[0] = jnp.sum(
            jnp.stack([summed[:, 128 * k : 128 * (k + 1)] for k in range(TILE // 128)]), axis=0
        )

    def sum_over_chips():
        for stage, dim in enumerate("zxy"):
            sent = [
                copies.send(squares.at[stage], square_parts.at[stage, slot], dim, step)
                for slot, step in enumerate((2, 1, 3))
            ]
            yield
            for copy in sent:
                copy.wait_recv()
            squares[stage + 1] = (squares[stage] + square_parts[stage, 0]) + (
                square_parts[stage, 1] + square_parts[stage, 2]
            )

    def rate():
        square_sum = jnp.sum(squares[3], axis=(0, 1), keepdims=True)
        return STEP_RATE / jnp.sqrt(square_sum / count_all + EPSILON)

    def update(iteration, step_rate, n, carry):
        at = pl.ds(pl.multiple_of(n * TILE, TILE), TILE)
        value = g_ref[n, :classes] + g_other[iteration, n, :classes]
        speed = MOMENTUM * v_ref[:, at] - step_rate * value
        v_ref[:, at] = speed
        w_ref[:, at] = w_ref[:, at] + speed
        return carry

    def loop(first, last, body):
        lax.fori_loop(first, last, body, 0)

    tiles = width // TILE
    score_tiles = frames // TILE
    half = score_tiles // CHUNKS

    copies = Copies(pos, send_sems, recv_sems, FRAME_COPIES)
    loop(0, tiles, functools.partial(look_ahead, MOMENTUM))
    loop(0, half, functools.partial(score, p_ref))
    early = advance_all(streams(0))
    loop(half, score_tiles - 1, functools.partial(score, p_ref))
    early = advance_all(early)
    loop(score_tiles - 1, score_tiles, functools.partial(score, p_ref))
    late = advance_all(streams(1))
    loop(0, tiles, functools.partial(look_ahead, MOMENTUM * (1.0 + MOMENTUM)))
    pending = [
        functools.partial(loop, n, n + 1, functools.partial(score, p_next))
        for n in range(score_tiles)
    ]
    finish_step(0, early, late, pending)

    copies.wait_sends()
    sum_squares(0, True)
    travel = sum_over_chips()
    for n in range(half):
        next(travel)
        loop(n, n + 1, functools.partial(score, p_ref))
    advance_all([travel])
    step_rate = rate()
    copies.wait_sends()
    for n in range(tiles):
        exchange(0, n).wait_send()
    copies = Copies(pos, send_sems, recv_sems, FRAME_COPIES)

    def combine(u, carry):
        p_ref[u] = p_next[u] - ((1.0 + MOMENTUM) * step_rate) * p_ref[u]
        return carry

    units = p_ref.shape[0]
    loop(0, units // CHUNKS, combine)
    early = advance_all(streams(0))
    loop(half, score_tiles - 1, functools.partial(score, p_ref))
    early = advance_all(early)
    loop(score_tiles - 1, score_tiles, functools.partial(score, p_ref))
    loop(units // CHUNKS, units, combine)
    late = advance_all(streams(1))
    pending = [functools.partial(loop, 0, tiles, functools.partial(update, 0, step_rate))]
    finish_step(1, early, late, pending)
    sum_squares(1, False)
    for _ in sum_over_chips():
        pass
    loop(0, tiles, functools.partial(update, 1, rate()))
    copies.wait_sends()
    for n in range(tiles):
        exchange(1, n).wait_send()


def on_device(frames, labels, proj, phase, class_weights, velocity):
    depth, width = proj.shape
    classes = class_weights.shape[1]
    feat_count = 64 * width
    scale = math.sqrt(2.0 / feat_count)
    count = labels.shape[0]
    f32, bf16 = jnp.float32, jnp.bfloat16
    units = count // 128 * 4
    colours = 3 * CHUNKS
    anywhere = pl.BlockSpec(memory_space=pl.ANY)
    vmem = pl.BlockSpec(memory_space=pltpu.VMEM)
    shape = jax.ShapeDtypeStruct((classes, width), f32)
    weights, speed = pl.pallas_call(
        functools.partial(kernel, scale, feat_count * classes),
        out_shape=[shape, shape],
        in_specs=[anywhere, vmem, anywhere, vmem, anywhere, anywhere],
        out_specs=[vmem, vmem],
        scratch_shapes=[
            pltpu.VMEM((count // 128, 128), f32),
            pltpu.VMEM(frames.shape, f32),
            pltpu.VMEM((4, 4, 4, frames.shape[0], 512), f32),
            pltpu.VMEM((depth, width), f32),
            pltpu.VMEM((512, width), bf16),
            pltpu.VMEM((512, width), bf16),
            pltpu.VMEM((count, width), bf16),
            pltpu.VMEM((count, width), bf16),
            pltpu.VMEM((2 * CLASS_PAD, width), bf16),
            pltpu.VMEM((units, UNIT, 128), f32),
            pltpu.VMEM((units, UNIT, 128), f32),
            pltpu.VMEM((units, UNIT, 128), f32),
            pltpu.VMEM((colours, 3, 4, UNIT, 128), f32),
            pltpu.VMEM((colours, 4, UNIT, 128), f32),
            pltpu.VMEM((colours, 3, UNIT, 128), f32),
            pltpu.VMEM((colours, UNIT, 128), f32),
            pltpu.VMEM((colours, 3, UNIT, 128), f32),
            pltpu.VMEM((2 * CLASS_PAD, count), bf16),
            pltpu.VMEM((width // TILE, CLASS_PAD, TILE), f32),
            pltpu.VMEM((ITERS, width // TILE, CLASS_PAD, TILE), f32),
            pltpu.VMEM((4, 8, 128), f32),
            pltpu.VMEM((3, 3, 8, 128), f32),
            pltpu.SemaphoreType.DMA((FRAME_COPIES + SCORE_COPIES + SQUARE_COPIES,)),
            pltpu.SemaphoreType.DMA((FRAME_COPIES + SCORE_COPIES + SQUARE_COPIES,)),
            pltpu.SemaphoreType.DMA((width // TILE,)),
            pltpu.SemaphoreType.DMA((ITERS, width // TILE)),
            pltpu.SemaphoreType.DMA((4,)),
        ],
        compiler_params=pltpu.CompilerParams(
            collective_id=0, has_side_effects=True, vmem_limit_bytes=VMEM_LIMIT
        ),
        name="optimize",
    )(frames, labels.reshape(count // 128, 128), proj, phase.reshape(1, width), class_weights.T, velocity.T)
    return weights.T, speed.T


def solution(mesh):
    return jax.shard_map(
        on_device,
        mesh=mesh,
        in_specs=(
            P(("frame", "feat"), None),
            P("frame"),
            P(None, "feat"),
            P("feat"),
            P("feat", None),
            P("feat", None),
        ),
        out_specs=(P("feat", None), P("feat", None)),
        check_vma=False,
    )
```
